32 devices in a mesh: grp: 2 (over x), lon: 8 (over z, y), lat: 2 (over core).
Axes of the slice: x: 2, y: 2, z: 4, core: 2. Of those that a mesh axis runs over, the one named last changes fastest.
Arguments:
- cloud_state: float32 [4, 256, 128, 1024], P('grp', 'lon', 'lat'), parts along dimension 0, may hold values from -6 to 6
- counts: int32 [512, 128], P(('grp', 'lon'), 'lat'), parts along dimension 0, may hold values from 1 to 8, as said below
- courant: float32 [32], replicated, may hold values from 0.2 to 0.9
- truncation: int32 [96], replicated, may hold values from 0 to 94, as said below
Outputs:
- cloud_next: float32 [4, 256, 128, 1024], P('grp', 'lon', 'lat'), parts along dimension 0
The draws below stay inside these ranges and needn't reach their ends.
There are 2 independent parts, one for each index of `grp`. The reference program is written for one: setup_inputs(seed, part) draws one part's arguments, and reference() takes and returns one part's arrays. A program takes and returns all parts, laid end to end along the dimension named above; an argument that names none is the same for every part. Nothing has to cross between parts.
Inputs may be any that keep to these rules, and one draw needn't show every extreme that they name: `counts`: columns come in busy regions of 4 to 8 substeps and calm ones of 1 or 2; column 0, 0 has 8. truncation[m] lies in m .. 85 for m <= 85, truncation[0] = 85, and truncation[m] = m - 1 (nothing kept) for m > 85.
All inputs are finite; a program needn't handle non-finite values.
Results may differ from the reference program's by a relative error of at most 0.0003.
Values sent between devices are 32-bit elements; how exact they have to be, the bound alone decides.
No kernel may reach another device: no remote copies, remote signals or barrier semaphores. Data moves between devices by JAX's collectives and lax.ppermute only.
A program may use at most 64 MiB of HBM per device.

```python
import jax
import jax.numpy as jnp
from jax import lax

NLON = 256
NLAT = 128
NCX = 32
NLEV = 32
MW = 96
NN = 96
NT = 85
SMAX = 8


def draw_counts(key, part):
    keys = jax.random.split(key, 4)
    lon_rows = jnp.arange(NLON)[:, None]
    lat_rows = jnp.arange(NLAT)[None, :]
    region = lon_rows // (NLON // 16) * 2 + lat_rows // (NLAT // 2)
    intensity = jax.random.randint(keys[0], (32,), 0, 5)
    group = lon_rows // max(NLON // 128, 1) * 2 + lat_rows // (NLAT // 2)
    chance = jax.random.randint(keys[1], (256,), 0, 4)
    stormy = chance[group] < intensity[region]
    busy = jax.random.randint(keys[2], (NLON, NLAT), 4, SMAX + 1)
    entries = jax.random.randint(keys[3], (NLON, NLAT), 1, 3)
    values = jnp.where(stormy, busy, entries)
    return values.at[0, 0].set(SMAX).astype(jnp.int32)


def draw_truncation(key, part):
    modes = jnp.arange(MW)
    lowest = jnp.minimum(modes, NT)
    drawn = jax.random.randint(key, (MW,), lowest, NT + 1)
    values = jnp.where(modes <= NT, drawn, modes - 1)
    return values.at[0].set(NT).astype(jnp.int32)


def block_scale(own_key, extent, pieces, low, high):
    gain, own = 1.0, jax.random.fold_in(own_key, 6)
    for axis_at, shards_of in pieces:
        heights = jnp.exp(jax.random.uniform(jax.random.fold_in(own, axis_at), (shards_of,), jnp.float32, low / len(pieces), high / len(pieces)))
        gain = gain * jnp.repeat(heights, extent[axis_at] // shards_of).reshape([-1 if axis == axis_at else 1 for axis in range(len(extent))])
    return gain


def gaussian(own_key, dims, deviation, most, shards=(), held_as=jnp.bfloat16):
    loudness = block_scale(own_key, dims, shards, -0.22, 0.18) if shards else 1.0
    entries = jax.random.normal(own_key, dims, jnp.float32) * deviation * loudness
    return jnp.minimum(jnp.maximum(entries, -most), most).astype(held_as)


def setup_inputs(seed: int = 0, part: int = 0) -> dict:
    seeds = jax.random.split(jax.random.key(seed), 5)
    part_splits = jax.random.split(jax.random.fold_in(seeds[4], part), 5)
    cloud_state = gaussian(part_splits[0], (2, NLON, NLAT, NCX * NLEV), 1.0, 6.0, ((1, 8), (2, 2)), jnp.float32)
    counts = draw_counts(jax.random.fold_in(jax.random.fold_in(seeds[4], part), 71), part)
    courant = jnp.clip(jax.random.uniform(seeds[2], (NLEV,), jnp.float32, 0.2, 0.9), 0.2, 0.9)
    truncation = draw_truncation(jax.random.fold_in(seeds[4], 71), part)
    return dict(cloud_state=cloud_state, counts=counts, courant=courant, truncation=truncation)


couple_gain = 8.0

def legendre(orders, lat_rows, lat_total, degrees):
    latitude = -0.5 * jnp.pi + jnp.pi * (lat_rows.astype(jnp.float32) + 0.5) / lat_total
    sin_lat = jnp.sin(latitude)
    cos_lat = jnp.cos(latitude)
    order_f = orders.astype(jnp.float32)
    ladder = jnp.arange(1, degrees + 1).astype(jnp.float32)
    log_gains = 0.5 * jnp.log((2.0 * ladder + 1.0) / (2.0 * ladder))
    included = (ladder[None, :] <= order_f[:, None]).astype(jnp.float32)
    log_start = 0.5 * jnp.log(jnp.float32(0.5)) + lax.optimization_barrier(jnp.sum(included * log_gains[None, :], axis=1))
    diagonal = jnp.exp(log_start[:, None] + order_f[:, None] * jnp.log(cos_lat)[None, :])

    def advance(carry, degree):
        previous, earlier, inverse = carry
        degree_f = degree.astype(jnp.float32)
        higher = degree_f > order_f
        numerator = jnp.maximum(4.0 * degree_f * degree_f - 1.0, 1.0)
        denominator = jnp.where(higher, degree_f * degree_f - order_f * order_f, 1.0)
        factor = jnp.sqrt(numerator / denominator)
        raised = factor[:, None] * (sin_lat[None, :] * previous - inverse[:, None] * earlier)
        current = jnp.where((degree_f == order_f)[:, None], diagonal, jnp.where(higher[:, None], raised, 0.0))
        return ((current, previous, jnp.where(higher, 1.0 / factor, 0.0)), current)
    initial = (jnp.zeros_like(diagonal), jnp.zeros_like(diagonal), jnp.zeros_like(order_f))
    _, stacked = lax.scan(advance, initial, jnp.arange(degrees, dtype=jnp.int32), unroll=8)
    return jnp.transpose(stacked, (1, 0, 2))

def latitude_weights(lat_rows, lat_total):
    latitude = -0.5 * jnp.pi + jnp.pi * (lat_rows.astype(jnp.float32) + 0.5) / lat_total
    return jnp.pi * jnp.cos(latitude) / lat_total

def wave_table(lon_rows, modes, lon_total):
    phase = lon_rows[:, None] * modes[None, :] % lon_total
    angle = phase.astype(jnp.float32) * (2.0 * jnp.pi / lon_total)
    return (jnp.cos(angle), jnp.sin(angle))

def substep(theta, moist, force, count, index, rate, profile, levels):
    heated = theta + couple_gain * profile[None, None, :] * force[:, :, None]
    moved_theta = heated - rate * (heated - jnp.roll(heated, levels, axis=2))
    moved_moist = moist - rate * (moist - jnp.roll(moist, levels, axis=2))
    excess = moved_moist - (1.0 + 0.2 * moved_theta)
    condensed = 0.25 * (excess + jnp.sqrt(excess * excess + 0.01))
    active = (index < count)[:, :, None]
    return (jnp.where(active, moved_theta + 0.5 * condensed, theta), jnp.where(active, moved_moist - condensed, moist))

def reference(cloud_state, counts, courant, truncation):
    highest = lax.Precision.HIGHEST
    heating = lax.optimization_barrier(jnp.mean(cloud_state[0], axis=2))
    lon_rows = jnp.arange(NLON, dtype=jnp.int32)
    modes = jnp.arange(MW, dtype=jnp.int32)
    cosine_table, sine_table = wave_table(lon_rows, modes, NLON)
    coefs = jnp.stack([jnp.dot(cosine_table.T, heating, precision=highest), jnp.dot(sine_table.T, heating, precision=highest)], 1) / NLON
    lat_rows = jnp.arange(NLAT, dtype=jnp.int32)
    table = legendre(modes, lat_rows, NLAT, NN)
    weights = latitude_weights(lat_rows, NLAT)
    spectrum = jnp.einsum('mnj,mcj->mcn', table, coefs * weights[None, None, :], precision=highest)
    degrees = jnp.arange(NN, dtype=jnp.int32)
    keep_mask = ((degrees[None, :] >= modes[:, None]) & (degrees[None, :] <= truncation[:, None])).astype(jnp.float32)
    filtered = jnp.einsum('mnj,mcn->mcj', table, spectrum * keep_mask[:, None, :], precision=highest)
    factor = jnp.where(modes == 0, 1.0, 2.0).astype(jnp.float32)[:, None]
    forcing = jnp.dot(cosine_table, factor * filtered[:, 0], precision=highest) + jnp.dot(sine_table, factor * filtered[:, 1], precision=highest)
    level_profile = jnp.sin(jnp.pi * (jnp.arange(NLEV).astype(jnp.float32) + 0.5) / NLEV)
    profile = jnp.tile(level_profile, NCX)
    rate = jnp.tile(courant, NCX)[None, None, :]
    theta = cloud_state[0]
    moist = cloud_state[1]
    for substep_index in range(SMAX):
        theta, moist = substep(theta, moist, forcing, counts, substep_index, rate, profile, NLEV)
    return jnp.stack([theta, moist])
```

```python
import jax
import jax.numpy as jnp
from jax import lax
from jax.experimental import pallas as pl
from jax.experimental.pallas import tpu as pltpu
from jax.sharding import PartitionSpec as P

NN = 96
couple_gain = 8.0
LANES = 128
HIGH = lax.Precision.HIGHEST
ALPHA = 0.275


def gather_heating(heating, lon_devices):
    other = lax.ppermute(heating, "lat", [(0, 1), (1, 0)])
    held = jnp.stack([heating, other])[:, None]
    step = 1
    while step < lon_devices:
        pairs = [(i, i ^ step) for i in range(lon_devices)]
        held = jnp.concatenate([held, lax.ppermute(held, "lon", pairs)], 1)
        step *= 2
    return held


def contract(a, b, dims):
    return lax.dot_general(a, b, (dims, ((), ())), precision=HIGH, preferred_element_type=jnp.float32)


def spectral_kernel(where_ref, held_ref, trunc_ref, out_ref, table, partial):
    lon_devices, lon_local, lat_local = held_ref.shape[1:]
    lon_index = where_ref[0]
    lat_index = where_ref[1]
    total_lon = lon_devices * lon_local
    total_lat = 2 * lat_local
    total_modes = where_ref.shape[0] - 2
    modes = lax.broadcasted_iota(jnp.int32, (1, LANES), 1)
    modes_f = modes.astype(jnp.float32)

    row = lax.broadcasted_iota(jnp.int32, (total_lon, LANES), 0)
    lane = lax.broadcasted_iota(jnp.int32, (total_lon, LANES), 1)
    source = (row // lon_local) ^ lon_index
    lon_row = source * lon_local + row % lon_local
    phase = lon_row * lane % total_lon
    angle = phase.astype(jnp.float32) * (2.0 * jnp.pi / total_lon)
    carried = (lane < total_modes).astype(jnp.float32)
    waves = jnp.concatenate([jnp.cos(angle) * carried, jnp.sin(angle) * carried], axis=1)

    rows = (lat_index * lat_local + lax.broadcasted_iota(jnp.int32, (lat_local, 1), 0)).astype(jnp.float32)
    latitude = -0.5 * jnp.pi + jnp.pi * (rows + 0.5) / total_lat
    sin_lat = jnp.broadcast_to(jnp.sin(latitude), (lat_local, LANES))
    cos_lat = jnp.cos(latitude)
    weight = jnp.pi * cos_lat / total_lat / total_lon

    mine = contract(held_ref[0].reshape(total_lon, lat_local), waves, ((0,), (0,)))
    others = contract(held_ref[1].reshape(total_lon, lat_local), waves, ((0,), (0,)))
    r = lax.broadcasted_iota(jnp.int32, (lat_local, lat_local), 0)
    c = lax.broadcasted_iota(jnp.int32, (lat_local, lat_local), 1)
    flip = (r + c == lat_local - 1).astype(jnp.float32)
    others = contract(flip, others, ((1,), (0,)))
    same = (mine + others) * weight
    diff = (mine - others) * weight
    lane2 = lax.broadcasted_iota(jnp.int32, (1, 2 * LANES), 1)
    even_mode = lane2 % 2 == 0
    folded = [jnp.where(even_mode, same, diff), jnp.where(even_mode, diff, same)]

    ladder = (lax.broadcasted_iota(jnp.int32, (NN, LANES), 0) + 1).astype(jnp.float32)
    gains = 0.5 * jnp.log((2.0 * ladder + 1.0) / (2.0 * ladder))
    log_start = 0.5 * jnp.log(jnp.float32(0.5)) + jnp.sum(
        jnp.where(ladder <= modes_f, gains, 0.0), axis=0, keepdims=True
    )
    diagonal = jnp.exp(log_start + modes_f * jnp.log(cos_lat))
    degree = lax.broadcasted_iota(jnp.int32, (NN, LANES), 0).astype(jnp.float32)

    def factor_of(degree_f):
        higher = degree_f > modes_f
        numerator = jnp.maximum(4.0 * degree_f * degree_f - 1.0, 1.0)
        denominator = jnp.where(higher, degree_f * degree_f - modes_f * modes_f, 1.0)
        return higher, jnp.sqrt(numerator / denominator)

    higher, factor = factor_of(degree)
    factor = jnp.where(higher, factor, 0.0)
    below, lower_factor = factor_of(degree - 1.0)
    ratio = jnp.where(below, factor / lower_factor, 0.0)

    previous = jnp.zeros((lat_local, LANES), jnp.float32)
    earlier = jnp.zeros((lat_local, LANES), jnp.float32)
    for n in range(NN):
        raised = factor[n : n + 1] * (sin_lat * previous) - ratio[n : n + 1] * earlier
        current = jnp.where(modes == n, diagonal, raised)
        table[n] = current
        for part in range(2):
            terms = current * folded[n % 2][:, part * LANES : (part + 1) * LANES]
            partial[part, n] = sum(terms[8 * i : 8 * i + 8] for i in range(lat_local // 8))
        previous, earlier = current, previous

    degree_i = lax.broadcasted_iota(jnp.int32, (NN, LANES), 0)
    keep = (degree_i >= modes) & (degree_i <= trunc_ref[0:1, :])
    scale = jnp.where(modes == 0, 1.0, 2.0)
    filtered = []
    for part in range(2):
        spectrum = jnp.where(keep, jnp.sum(partial[part], axis=1) * scale, 0.0)
        total = jnp.zeros((lat_local, LANES), jnp.float32)
        for n in range(NN):
            total = total + table[n] * spectrum[n : n + 1]
        filtered.append(total)
    filtered = jnp.concatenate(filtered, axis=1)
    forcing = contract(filtered, waves[:lon_local], ((1,), (1,)))
    for l in range(lon_local):
        out_ref[l] = jnp.broadcast_to(forcing[:, l : l + 1], (lat_local, LANES))


def cloud_kernel(state_ref, forcing_ref, counts_ref, rate_ref, profile_ref, out_ref):
    lon_block, lat_local, cells = state_ref.shape[1:]
    pieces = cells // LANES
    levels = LANES // 4
    group = 4
    keep_rate = (1.0 - rate_ref[...]) * ALPHA
    move_rate = rate_ref[...] * ALPHA
    lane = lax.broadcasted_iota(jnp.int32, (8, LANES), 1)
    first = lane < levels
    gain = 0.725 / ALPHA
    floor = ALPHA * ALPHA * 0.01

    def body(index, carry):
        columns = []
        for g in range(group):
            row = pl.ds(pl.multiple_of((index * group + g) * 8, 8), 8)
            theta = [state_ref[0, 0, row, pl.ds(LANES * v, LANES)] for v in range(pieces)]
            moist = [state_ref[1, 0, row, pl.ds(LANES * v, LANES)] for v in range(pieces)]
            push = couple_gain * profile_ref[...] * forcing_ref[0, row, :]
            columns.append((row, theta, moist, push, counts_ref[0, row, :]))

        def step(s, carry):
            out = []
            for (row, _, _, push, count), (z, w) in zip(columns, carry):
                active = s < count
                new_z, new_w = [], []
                dry = [x + push for x in z]
                turn_z = [pltpu.roll(x, levels, 1) for x in dry]
                turn_w = [pltpu.roll(x, levels, 1) for x in w]
                for v in range(pieces):
                    back = jnp.where(first, turn_z[v - 1], turn_z[v])
                    new_z.append(jnp.where(active, dry[v] + rate_ref[...] * (back - dry[v]), z[v]))
                    back = jnp.where(first, turn_w[v - 1], turn_w[v])
                    e = keep_rate * w[v] + move_rate * back - (0.2 * ALPHA) * push
                    y = e * e + floor
                    new_w.append(jnp.where(active, gain * e - y * lax.rsqrt(y), w[v]))
                out.append((new_z, new_w))
            return out

        start = [
            ([t + 0.5 * m for t, m in zip(theta, moist)], [m - 0.2 * t - 1.0 for t, m in zip(theta, moist)])
            for _, theta, moist, _, _ in columns
        ]
        most = jnp.max(jnp.maximum(jnp.maximum(columns[0][4], columns[1][4]), jnp.maximum(columns[2][4], columns[3][4])))
        done = lax.fori_loop(0, most, step, start)
        for (row, _, _, _, _), (z, w) in zip(columns, done):
            for v in range(pieces):
                theta = (z[v] - 0.5 * w[v] - 0.5) * (1.0 / 1.1)
                out_ref[0, 0, row, pl.ds(LANES * v, LANES)] = theta
                out_ref[1, 0, row, pl.ds(LANES * v, LANES)] = w[v] + 1.0 + 0.2 * theta
        return carry

    lax.fori_loop(0, lat_local // (8 * group), body, 0)


def shards(cloud_state, counts, courant, truncation):
    lon_devices = lax.axis_size("lon")
    fields, lon_local, lat_local, cells = cloud_state.shape
    levels = courant.shape[0]
    total_modes = truncation.shape[0]
    heating = jnp.mean(cloud_state[0], axis=2)
    held = gather_heating(heating, lon_devices)
    where = jnp.concatenate(
        [jnp.stack([lax.axis_index("lon"), lax.axis_index("lat")]).astype(jnp.int32), jnp.zeros((total_modes,), jnp.int32)]
    )
    trunc = jnp.broadcast_to(jnp.pad(truncation, (0, LANES - total_modes), constant_values=-1)[None], (8, LANES))
    vmem = pl.BlockSpec(memory_space=pltpu.VMEM)
    forcing = pl.pallas_call(
        spectral_kernel,
        in_specs=[pl.BlockSpec(memory_space=pltpu.SMEM), vmem, vmem],
        out_specs=vmem,
        out_shape=jax.ShapeDtypeStruct((lon_local, lat_local, LANES), jnp.float32),
        scratch_shapes=[
            pltpu.VMEM((NN, lat_local, LANES), jnp.float32),
            pltpu.VMEM((2, NN, 8, LANES), jnp.float32),
        ],
        compiler_params=pltpu.CompilerParams(vmem_limit_bytes=48 << 20),
        name="spectral",
    )(where, held, trunc)
    level_profile = jnp.sin(jnp.pi * (jnp.arange(levels).astype(jnp.float32) + 0.5) / levels)
    profile = jnp.tile(level_profile, LANES // levels)[None]
    rate = jnp.tile(courant, LANES // levels)[None]
    count_rows = jnp.broadcast_to(counts[:, :, None], (lon_local, lat_local, LANES))
    state_spec = pl.BlockSpec((fields, 1, lat_local, cells), lambda i: (0, i, 0, 0))
    row_spec = pl.BlockSpec((1, lat_local, LANES), lambda i: (i, 0, 0))
    return pl.pallas_call(
        cloud_kernel,
        grid=(lon_local,),
        in_specs=[state_spec, row_spec, row_spec, vmem, vmem],
        out_specs=state_spec,
        out_shape=jax.ShapeDtypeStruct(cloud_state.shape, jnp.float32),
        name="clouds",
    )(cloud_state, forcing, count_rows, rate, profile)


def solution(mesh):
    return jax.shard_map(
        shards,
        mesh=mesh,
        in_specs=(P("grp", "lon", "lat", None), P(("grp", "lon"), "lat"), P(), P()),
        out_specs=P("grp", "lon", "lat", None),
        check_vma=False,
    )
```

```python
import math

import jax
import jax.numpy as jnp
from jax import lax
from jax.experimental import pallas as pl
from jax.experimental.pallas import tpu as pltpu
from jax.sharding import PartitionSpec as P

NN = 96
couple_gain = 8.0
LANES = 128
HIGH = lax.Precision.HIGHEST
ALPHA = 0.275


def gather_heating(heating, lon_devices):
    other = lax.ppermute(heating, "lat", [(0, 1), (1, 0)])
    held = jnp.stack([heating, other])[:, None]
    step = 1
    while step < lon_devices:
        pairs = [(i, i ^ step) for i in range(lon_devices)]
        held = jnp.concatenate([held, lax.ppermute(held, "lon", pairs)], 1)
        step *= 2
    return held


def contract(a, b, dims):
    return lax.dot_general(a, b, (dims, ((), ())), precision=HIGH, preferred_element_type=jnp.float32)


def spectral_kernel(where_ref, held_ref, trunc_ref, courant_ref, out_ref, table, partial, limit):
    lon_devices, lon_local, lat_local = held_ref.shape[1:]
    lon_index = where_ref[0]
    lat_index = where_ref[1]
    total_lon = lon_devices * lon_local
    total_lat = 2 * lat_local
    total_modes = trunc_ref.shape[1]
    modes = lax.broadcasted_iota(jnp.int32, (1, LANES), 1)
    modes_f = modes.astype(jnp.float32)

    row = lax.broadcasted_iota(jnp.int32, (total_lon, LANES), 0)
    lane = lax.broadcasted_iota(jnp.int32, (total_lon, LANES), 1)
    source = (row // lon_local) ^ lon_index
    lon_row = source * lon_local + row % lon_local
    phase = lon_row * lane % total_lon
    angle = phase.astype(jnp.float32) * (2.0 * jnp.pi / total_lon)
    carried = (lane < total_modes).astype(jnp.float32)
    waves = jnp.concatenate([jnp.cos(angle) * carried, jnp.sin(angle) * carried], axis=1)

    rows = (lat_index * lat_local + lax.broadcasted_iota(jnp.int32, (lat_local, 1), 0)).astype(jnp.float32)
    latitude = -0.5 * jnp.pi + jnp.pi * (rows + 0.5) / total_lat
    sin_lat = jnp.broadcast_to(jnp.sin(latitude), (lat_local, LANES))
    cos_lat = jnp.cos(latitude)
    weight = jnp.pi * cos_lat / total_lat / total_lon

    mine = contract(held_ref[0].reshape(total_lon, lat_local), waves, ((0,), (0,)))
    others = contract(held_ref[1].reshape(total_lon, lat_local), waves, ((0,), (0,)))
    r = lax.broadcasted_iota(jnp.int32, (lat_local, lat_local), 0)
    c = lax.broadcasted_iota(jnp.int32, (lat_local, lat_local), 1)
    flip = (r + c == lat_local - 1).astype(jnp.float32)
    others = contract(flip, others, ((1,), (0,)))
    same = (mine + others) * weight
    diff = (mine - others) * weight
    lane2 = lax.broadcasted_iota(jnp.int32, (1, 2 * LANES), 1)
    even_mode = lane2 % 2 == 0
    folded = [jnp.where(even_mode, same, diff), jnp.where(even_mode, diff, same)]

    ladder = (lax.broadcasted_iota(jnp.int32, (NN, LANES), 0) + 1).astype(jnp.float32)
    gains = 0.5 * jnp.log((2.0 * ladder + 1.0) / (2.0 * ladder))
    log_start = 0.5 * jnp.log(jnp.float32(0.5)) + jnp.sum(
        jnp.where(ladder <= modes_f, gains, 0.0), axis=0, keepdims=True
    )
    diagonal = jnp.exp(log_start + modes_f * jnp.log(cos_lat))
    degree = lax.broadcasted_iota(jnp.int32, (NN, LANES), 0).astype(jnp.float32)

    def factor_of(degree_f):
        higher = degree_f > modes_f
        numerator = jnp.maximum(4.0 * degree_f * degree_f - 1.0, 1.0)
        denominator = jnp.where(higher, degree_f * degree_f - modes_f * modes_f, 1.0)
        return higher, jnp.sqrt(numerator / denominator)

    higher, factor = factor_of(degree)
    factor = jnp.where(higher, factor, 0.0)
    below, lower_factor = factor_of(degree - 1.0)
    ratio = jnp.where(below, factor / lower_factor, 0.0)

    previous = jnp.zeros((lat_local, LANES), jnp.float32)
    earlier = jnp.zeros((lat_local, LANES), jnp.float32)
    for n in range(NN):
        raised = factor[n : n + 1] * (sin_lat * previous) - ratio[n : n + 1] * earlier
        current = jnp.where(modes == n, diagonal, raised)
        table[n] = current
        for part in range(2):
            terms = current * folded[n % 2][:, part * LANES : (part + 1) * LANES]
            partial[part, n] = sum(terms[8 * i : 8 * i + 8] for i in range(lat_local // 8))
        previous, earlier = current, previous

    limit[...] = jnp.full((1, LANES), -1, jnp.int32)
    limit[:, :total_modes] = trunc_ref[...]
    degree_i = lax.broadcasted_iota(jnp.int32, (NN, LANES), 0)
    keep = (degree_i >= modes) & (degree_i <= limit[...])
    scale = jnp.where(modes == 0, 1.0, 2.0)
    filtered = []
    for part in range(2):
        spectrum = jnp.where(keep, jnp.sum(partial[part], axis=1) * scale, 0.0)
        total = jnp.zeros((lat_local, LANES), jnp.float32)
        for n in range(NN):
            total = total + table[n] * spectrum[n : n + 1]
        filtered.append(total)
    filtered = jnp.concatenate(filtered, axis=1)
    forcing = contract(filtered, waves[:lon_local], ((1,), (1,)))
    level = lax.broadcasted_iota(jnp.int32, (1, LANES), 1) % courant_ref.shape[1]
    profile = couple_gain * jnp.sin(jnp.pi * (level.astype(jnp.float32) + 0.5) / courant_ref.shape[1])
    for l in range(lon_local):
        out_ref[l * lat_local : (l + 1) * lat_local] = forcing[:, l : l + 1] * profile


GROUP = 16
QUADS = GROUP // 4
TOP = 8


def order_kernel(counts_ref, column_ref, row_ref, bound_ref):
    lon_local, lat_local = counts_ref.shape
    chunks = column_ref.shape[0] // 8
    chunk_lon = lon_local // chunks
    counts = counts_ref[...]
    rows = TOP * lon_local
    masks = [jnp.where(counts == n + 1, 1.0, 0.0) for n in range(TOP)]
    mask = jnp.concatenate(masks, axis=0).astype(jnp.bfloat16)

    def dot(a, b):
        return lax.dot_general(a.astype(jnp.bfloat16), b.astype(jnp.bfloat16), (((1,), (0,)), ((), ())), preferred_element_type=jnp.float32)

    r = lax.broadcasted_iota(jnp.int32, (lat_local, lat_local), 0)
    c = lax.broadcasted_iota(jnp.int32, (lat_local, lat_local), 1)
    before = dot(mask, jnp.where(r < c, 1.0, 0.0))
    total = dot(mask, jnp.ones((lat_local, LANES), jnp.float32))
    r = lax.broadcasted_iota(jnp.int32, (rows, rows), 0)
    c = lax.broadcasted_iota(jnp.int32, (rows, rows), 1)
    r_class, r_lon, c_class, c_lon = r // lon_local, r % lon_local, c // lon_local, c % lon_local
    same_chunk = r_lon // chunk_lon == c_lon // chunk_lon
    same_class = (r_class == c_class) & same_chunk
    rank = before + dot(jnp.where(same_class & (c_lon < r_lon), 1.0, 0.0), total)[:, :lat_local]
    size = dot(jnp.where(same_class, 1.0, 0.0), total)
    size = jnp.floor((size + (GROUP - 1)) * (1.0 / GROUP)) * GROUP
    base = dot(jnp.where((c_class < r_class) & (c_lon == r_lon), 1.0, 0.0), size)
    place = rank + base[:, :lat_local]
    slot = jnp.zeros((lon_local, lat_local), jnp.float32)
    for n in range(TOP):
        slot = slot + masks[n] * place[n * lon_local : (n + 1) * lon_local]
    slot = slot.astype(jnp.int32)
    high, low = slot // LANES, slot % LANES
    high_index = lax.broadcasted_iota(jnp.int32, (8, lat_local), 0)
    low_index = lax.broadcasted_iota(jnp.int32, (LANES, lat_local), 0)
    lat = lax.broadcasted_iota(jnp.int32, (8, lat_local), 1).astype(jnp.float32)
    spare = lon_local * lat_local
    for k in range(chunks):
        found = jnp.zeros((8, LANES), jnp.float32)
        lon_sum = jnp.zeros((8, LANES), jnp.float32)
        lat_sum = jnp.zeros((8, LANES), jnp.float32)
        for l in range(k * chunk_lon, (k + 1) * chunk_lon):
            at_high = jnp.where(high[l : l + 1] == high_index, 1.0, 0.0)
            at_low = jnp.where(low[l : l + 1] == low_index, 1.0, 0.0)
            both = jnp.concatenate([at_high, at_high * lat], axis=0)
            hit = lax.dot_general(both.astype(jnp.bfloat16), at_low.astype(jnp.bfloat16), (((1,), (1,)), ((), ())), preferred_element_type=jnp.float32)
            found = found + hit[:8]
            lon_sum = lon_sum + hit[:8] * float(l)
            lat_sum = lat_sum + hit[8:]
        column = jnp.where(found > 0.5, lon_sum * lat_local + lat_sum, float(spare)).astype(jnp.int32)
        column_ref[8 * k : 8 * k + 8] = column
        row_ref[8 * k : 8 * k + 8] = column // 8 * 64 + column % 8
    row_index = lax.broadcasted_iota(jnp.int32, (rows, LANES), 0)
    lane = lax.broadcasted_iota(jnp.int32, (rows, LANES), 1)
    first = jnp.where(lane == row_index // lon_local, base, 0.0) + jnp.where(lane == TOP + row_index // lon_local, base + size, 0.0)
    bounds = []
    for k in range(8):
        bounds.append(jnp.sum(jnp.where(row_index % lon_local == min(k, chunks - 1) * chunk_lon, first, 0.0), axis=0, keepdims=True))
    bound_ref[...] = (jnp.concatenate(bounds, axis=0) * (1.0 / GROUP)).astype(jnp.int32)


def turn_quad(xs, low_half, even):
    a, b, c, d = xs
    roll = lambda x, s: pltpu.roll(x, s, 1)
    a, c = jnp.where(low_half, a, roll(c, 64)), jnp.where(low_half, roll(a, 64), c)
    b, d = jnp.where(low_half, b, roll(d, 64)), jnp.where(low_half, roll(b, 64), d)
    a, b = jnp.where(even, a, roll(b, 32)), jnp.where(even, roll(a, 96), b)
    c, d = jnp.where(even, c, roll(d, 32)), jnp.where(even, roll(c, 96), d)
    return [a, b, c, d]


def cloud_kernel(column_ref, row_ref, bound_ref, state_ref, forcing_ref, courant_ref, out_ref, taken, given, ready, mid, done, power, in_sem, out_sem):
    chunks = column_ref.shape[0] // 8
    chunk_rows = state_ref.shape[1] // chunks
    levels = courant_ref.shape[1]

    def fetch(k):
        rows = pl.ds(pl.multiple_of(k * chunk_rows, 8), chunk_rows)
        return pltpu.make_async_copy(state_ref.at[:, rows], taken.at[:, rows], in_sem.at[k])

    def send(k):
        rows = pl.ds(pl.multiple_of(k * chunk_rows, 8), chunk_rows)
        return pltpu.make_async_copy(given.at[:, rows], out_ref.at[:, rows], out_sem.at[k])

    for k in range(chunks):
        fetch(k).start()

    rate = jnp.concatenate([courant_ref[...]] * (LANES // levels), axis=1)
    rate = jnp.broadcast_to(rate, (8, LANES))
    stay = 1.0 - rate
    for n in range(1, TOP + 1):
        for j in range(n + 1):
            value = jnp.full((8, LANES), math.comb(n, j) / 1.1, jnp.float32)
            for _ in range(j):
                value = value * rate
            for _ in range(n - j):
                value = value * stay
            power[n * (TOP + 1) + j] = value

    lane = lax.broadcasted_iota(jnp.int32, (8, LANES), 1)
    low_half = lane < 64
    even = lane // 32 % 2 == 0

    def place(k, g):
        return k * 8 + g // 8, g % 8 * GROUP

    def load(k, g):
        top, left = place(k, g)
        for q in range(QUADS):
            dry, wet, push = [], [], []
            for c in range(4):
                row = row_ref[top, left + 4 * q + c]
                theta = taken[0, pl.ds(row, 8, stride=8), :]
                moist = taken[1, pl.ds(row, 8, stride=8), :]
                dry.append(theta + 0.5 * moist)
                wet.append(moist - 0.2 * theta)
                push.append(jnp.broadcast_to(forcing_ref[pl.ds(column_ref[top, left + 4 * q + c], 1), :], (8, LANES)))
            for u, x in enumerate(turn_quad(wet, low_half, even)):
                ready[q * 9 + u] = x
            for u, x in enumerate(turn_quad(dry, low_half, even)):
                ready[q * 9 + 4 + u] = x
            ready[q * 9 + 8] = jnp.where(low_half, jnp.where(even, push[0], push[1]), jnp.where(even, push[2], push[3]))

    keep_rate = stay * ALPHA
    move_rate = rate * ALPHA
    gain = 0.725 / ALPHA
    floor = ALPHA * ALPHA * 0.01

    def drift(n):
        for q in range(QUADS):
            dry = [[ready[q * 9 + 4 + u] for u in range(4)]]
            dry.append([pltpu.roll(x, 1, 0) for x in dry[0]])
            if n > 4:
                dry.append([pltpu.roll(x, 2, 0) for x in dry[0]])
            shift = (n / 1.1) * ready[q * 9 + 8] - 0.5 / 1.1
            for u in range(4):
                total = shift
                for j in range(n + 1):
                    wraps = (j - u + 3) // 4 if j > u else 0
                    total = total + power[n * (TOP + 1) + j] * dry[wraps][(u - j) % 4]
                mid[q * 4 + u] = total

    def react(n):
        wet = [[ready[q * 9 + u] for u in range(4)] for q in range(QUADS)]
        pull = [(0.2 * ALPHA) * ready[q * 9 + 8] for q in range(QUADS)]
        for s in range(n):
            for q in range(QUADS):
                w = wet[q]
                less = pull[q] + ALPHA if s == 0 else pull[q]
                back = [pltpu.roll(w[3], 1, 0), w[0], w[1], w[2]]
                fresh = []
                for u in range(4):
                    e = keep_rate * w[u] + move_rate * back[u] - less
                    y = e * e + floor
                    fresh.append(gain * e - y * lax.rsqrt(y))
                wet[q] = fresh
        return wet

    def finish(wet):
        for q in range(QUADS):
            for u in range(4):
                theta = mid[q * 4 + u] - (0.5 / 1.1) * wet[q][u]
                done[q * 8 + u] = theta
                done[q * 8 + 4 + u] = wet[q][u] + 1.0 + 0.2 * theta

    def store(k, g):
        top, left = place(k, g)
        for q in range(QUADS):
            for field in range(2):
                turned = turn_quad([done[q * 8 + 4 * field + u] for u in range(4)], low_half, even)
                for c in range(4):
                    row = row_ref[top, left + 4 * q + c]
                    given[field, pl.ds(row, 8, stride=8), :] = turned[c]

    fetch(0).wait()
    load(0, 0)

    def chunk(k, carry):
        @pl.when(k + 1 < chunks)
        def _():
            fetch(jnp.minimum(k + 1, chunks - 1)).wait()

        groups = bound_ref[k, 2 * TOP - 1]
        for n in range(1, TOP + 1):
            start, stop = bound_ref[k, n - 1], bound_ref[k, TOP + n - 1]

            def body(g, carry, n=n):
                last_k, last_g = carry
                over = g + 1 >= groups
                next_k = jnp.where(over, jnp.minimum(k + 1, chunks - 1), k)
                next_g = jnp.where(over, 0, g + 1)
                store(last_k, last_g)
                drift(n)
                wet = react(n)
                load(next_k, next_g)
                finish(wet)
                return k, g

            carry = lax.fori_loop(start, stop, body, carry)

            @pl.when((k > 0) & (start == 0) & (stop > 0))
            def _():
                send(jnp.maximum(k - 1, 0)).start()

        return carry

    last_k, last_g = lax.fori_loop(0, chunks, chunk, (jnp.int32(0), jnp.int32(63)))
    store(last_k, last_g)
    send(chunks - 1).start()
    for k in range(chunks):
        send(k).wait()


def shards(cloud_state, counts, courant, truncation):
    lon_devices = lax.axis_size("lon")
    fields, lon_local, lat_local, cells = cloud_state.shape
    levels = courant.shape[0]
    total_modes = truncation.shape[0]
    pieces = cells // LANES
    columns = lon_local * lat_local
    chunks = 4
    vmem = pl.BlockSpec(memory_space=pltpu.VMEM)
    smem = pl.BlockSpec(memory_space=pltpu.SMEM)
    column, row, bound = pl.pallas_call(
        order_kernel,
        in_specs=[vmem],
        out_specs=[vmem, vmem, vmem],
        out_shape=[
            jax.ShapeDtypeStruct((8 * chunks, LANES), jnp.int32),
            jax.ShapeDtypeStruct((8 * chunks, LANES), jnp.int32),
            jax.ShapeDtypeStruct((8, LANES), jnp.int32),
        ],
        name="order",
    )(counts)
    heating = jnp.mean(cloud_state[0], axis=2)
    held = gather_heating(heating, lon_devices)
    where = jnp.stack([lax.axis_index("lon"), lax.axis_index("lat")]).astype(jnp.int32)
    forcing = pl.pallas_call(
        spectral_kernel,
        in_specs=[smem, vmem, vmem, vmem],
        out_specs=vmem,
        out_shape=jax.ShapeDtypeStruct((columns + 8, LANES), jnp.float32),
        scratch_shapes=[
            pltpu.VMEM((NN, lat_local, LANES), jnp.float32),
            pltpu.VMEM((2, NN, 8, LANES), jnp.float32),
            pltpu.VMEM((1, LANES), jnp.int32),
        ],
        compiler_params=pltpu.CompilerParams(vmem_limit_bytes=48 << 20),
        name="spectral",
    )(where, held, truncation[None], courant[None])
    tiles = cloud_state.reshape(fields, lon_local, lat_local // 8, 8, pieces, LANES)
    tiles = tiles.transpose(0, 1, 2, 4, 3, 5).reshape(fields, columns * pieces, LANES)
    held_rows = columns * pieces + 8 * pieces
    out = pl.pallas_call(
        cloud_kernel,
        in_specs=[smem, smem, smem, pl.BlockSpec(memory_space=pl.ANY), vmem, vmem],
        out_specs=pl.BlockSpec(memory_space=pl.ANY),
        out_shape=jax.ShapeDtypeStruct(tiles.shape, jnp.float32),
        scratch_shapes=[
            pltpu.VMEM((fields, held_rows, LANES), jnp.float32),
            pltpu.VMEM((fields, held_rows, LANES), jnp.float32),
            pltpu.VMEM((QUADS * 9, 8, LANES), jnp.float32),
            pltpu.VMEM((QUADS * 4, 8, LANES), jnp.float32),
            pltpu.VMEM((QUADS * 8, 8, LANES), jnp.float32),
            pltpu.VMEM(((TOP + 1) ** 2, 8, LANES), jnp.float32),
            pltpu.SemaphoreType.DMA((chunks,)),
            pltpu.SemaphoreType.DMA((chunks,)),
        ],
        compiler_params=pltpu.CompilerParams(vmem_limit_bytes=60 << 20),
        name="clouds",
    )(column, row, bound, tiles, forcing, courant[None])
    out = out.reshape(fields, lon_local, lat_local // 8, pieces, 8, LANES)
    return out.transpose(0, 1, 2, 4, 3, 5).reshape(cloud_state.shape)


def solution(mesh):
    return jax.shard_map(
        shards,
        mesh=mesh,
        in_specs=(P("grp", "lon", "lat", None), P(("grp", "lon"), "lat"), P(), P()),
        out_specs=P("grp", "lon", "lat", None),
        check_vma=False,
    )
```

```python
import math

import jax
import jax.numpy as jnp
from jax import lax
from jax.experimental import pallas as pl
from jax.experimental.pallas import tpu as pltpu
from jax.sharding import PartitionSpec as P

NN = 96
couple_gain = 8.0
LANES = 128
HIGH = lax.Precision.HIGHEST
ALPHA = 0.275


def gather_heating(heating, lon_devices):
    other = lax.ppermute(heating, "lat", [(0, 1), (1, 0)])
    held = jnp.stack([heating, other])[:, None]
    step = 1
    while step < lon_devices:
        pairs = [(i, i ^ step) for i in range(lon_devices)]
        held = jnp.concatenate([held, lax.ppermute(held, "lon", pairs)], 1)
        step *= 2
    return held


def contract(a, b, dims):
    return lax.dot_general(a, b, (dims, ((), ())), precision=HIGH, preferred_element_type=jnp.float32)


def spectral_kernel(where_ref, held_ref, trunc_ref, courant_ref, out_ref, table, partial, limit):
    lon_devices, lon_local, lat_local = held_ref.shape[1:]
    lon_index = where_ref[0]
    lat_index = where_ref[1]
    total_lon = lon_devices * lon_local
    total_lat = 2 * lat_local
    total_modes = trunc_ref.shape[1]
    modes = lax.broadcasted_iota(jnp.int32, (1, LANES), 1)
    modes_f = modes.astype(jnp.float32)

    row = lax.broadcasted_iota(jnp.int32, (total_lon, LANES), 0)
    lane = lax.broadcasted_iota(jnp.int32, (total_lon, LANES), 1)
    source = (row // lon_local) ^ lon_index
    lon_row = source * lon_local + row % lon_local
    phase = lon_row * lane % total_lon
    angle = phase.astype(jnp.float32) * (2.0 * jnp.pi / total_lon)
    carried = (lane < total_modes).astype(jnp.float32)
    waves = jnp.concatenate([jnp.cos(angle) * carried, jnp.sin(angle) * carried], axis=1)

    rows = (lat_index * lat_local + lax.broadcasted_iota(jnp.int32, (lat_local, 1), 0)).astype(jnp.float32)
    latitude = -0.5 * jnp.pi + jnp.pi * (rows + 0.5) / total_lat
    sin_lat = jnp.broadcast_to(jnp.sin(latitude), (lat_local, LANES))
    cos_lat = jnp.cos(latitude)
    weight = jnp.pi * cos_lat / total_lat / total_lon

    mine = contract(held_ref[0].reshape(total_lon, lat_local), waves, ((0,), (0,)))
    others = contract(held_ref[1].reshape(total_lon, lat_local), waves, ((0,), (0,)))
    r = lax.broadcasted_iota(jnp.int32, (lat_local, lat_local), 0)
    c = lax.broadcasted_iota(jnp.int32, (lat_local, lat_local), 1)
    flip = (r + c == lat_local - 1).astype(jnp.float32)
    others = contract(flip, others, ((1,), (0,)))
    same = (mine + others) * weight
    diff = (mine - others) * weight
    lane2 = lax.broadcasted_iota(jnp.int32, (1, 2 * LANES), 1)
    even_mode = lane2 % 2 == 0
    folded = [jnp.where(even_mode, same, diff), jnp.where(even_mode, diff, same)]

    ladder = (lax.broadcasted_iota(jnp.int32, (NN, LANES), 0) + 1).astype(jnp.float32)
    gains = 0.5 * jnp.log((2.0 * ladder + 1.0) / (2.0 * ladder))
    log_start = 0.5 * jnp.log(jnp.float32(0.5)) + jnp.sum(
        jnp.where(ladder <= modes_f, gains, 0.0), axis=0, keepdims=True
    )
    diagonal = jnp.exp(log_start + modes_f * jnp.log(cos_lat))
    degree = lax.broadcasted_iota(jnp.int32, (NN, LANES), 0).astype(jnp.float32)

    def factor_of(degree_f):
        higher = degree_f > modes_f
        numerator = jnp.maximum(4.0 * degree_f * degree_f - 1.0, 1.0)
        denominator = jnp.where(higher, degree_f * degree_f - modes_f * modes_f, 1.0)
        return higher, jnp.sqrt(numerator / denominator)

    higher, factor = factor_of(degree)
    factor = jnp.where(higher, factor, 0.0)
    below, lower_factor = factor_of(degree - 1.0)
    ratio = jnp.where(below, factor / lower_factor, 0.0)

    previous = jnp.zeros((lat_local, LANES), jnp.float32)
    earlier = jnp.zeros((lat_local, LANES), jnp.float32)
    for n in range(NN):
        raised = factor[n : n + 1] * (sin_lat * previous) - ratio[n : n + 1] * earlier
        current = jnp.where(modes == n, diagonal, raised)
        table[n] = current
        for part in range(2):
            terms = current * folded[n % 2][:, part * LANES : (part + 1) * LANES]
            partial[part, n] = sum(terms[8 * i : 8 * i + 8] for i in range(lat_local // 8))
        previous, earlier = current, previous

    limit[...] = jnp.full((1, LANES), -1, jnp.int32)
    limit[:, :total_modes] = trunc_ref[...]
    degree_i = lax.broadcasted_iota(jnp.int32, (NN, LANES), 0)
    keep = (degree_i >= modes) & (degree_i <= limit[...])
    scale = jnp.where(modes == 0, 1.0, 2.0)
    filtered = []
    for part in range(2):
        spectrum = jnp.where(keep, jnp.sum(partial[part], axis=1) * scale, 0.0)
        total = jnp.zeros((lat_local, LANES), jnp.float32)
        for n in range(NN):
            total = total + table[n] * spectrum[n : n + 1]
        filtered.append(total)
    filtered = jnp.concatenate(filtered, axis=1)
    forcing = contract(filtered, waves[:lon_local], ((1,), (1,)))
    level = lax.broadcasted_iota(jnp.int32, (1, LANES), 1) % courant_ref.shape[1]
    profile = couple_gain * jnp.sin(jnp.pi * (level.astype(jnp.float32) + 0.5) / courant_ref.shape[1])
    for l in range(lon_local):
        out_ref[l * lat_local : (l + 1) * lat_local] = forcing[:, l : l + 1] * profile


GROUP = 16
QUADS = GROUP // 4
TOP = 8


def order_kernel(counts_ref, column_ref, row_ref, bound_ref):
    lon_local, lat_local = counts_ref.shape
    chunks = bound_ref.shape[0]
    chunk_lon = lon_local // chunks
    counts = counts_ref[...]
    rows = TOP * lon_local
    masks = [jnp.where(counts == n + 1, 1.0, 0.0) for n in range(TOP)]
    mask = jnp.concatenate(masks, axis=0).astype(jnp.bfloat16)

    def dot(a, b):
        return lax.dot_general(a.astype(jnp.bfloat16), b.astype(jnp.bfloat16), (((1,), (0,)), ((), ())), preferred_element_type=jnp.float32)

    r = lax.broadcasted_iota(jnp.int32, (lat_local, lat_local), 0)
    c = lax.broadcasted_iota(jnp.int32, (lat_local, lat_local), 1)
    before = dot(mask, jnp.where(r < c, 1.0, 0.0))
    total = dot(mask, jnp.ones((lat_local, LANES), jnp.float32))
    r = lax.broadcasted_iota(jnp.int32, (rows, rows), 0)
    c = lax.broadcasted_iota(jnp.int32, (rows, rows), 1)
    r_class, r_lon, c_class, c_lon = r // lon_local, r % lon_local, c // lon_local, c % lon_local
    same_chunk = r_lon // chunk_lon == c_lon // chunk_lon
    same_class = (r_class == c_class) & same_chunk
    rank = before + dot(jnp.where(same_class & (c_lon < r_lon), 1.0, 0.0), total)[:, :lat_local]
    size = dot(jnp.where(same_class, 1.0, 0.0), total)
    size = jnp.floor((size + (GROUP - 1)) * (1.0 / GROUP)) * GROUP
    ahead = (c_lon // chunk_lon < r_lon // chunk_lon) | (same_chunk & (c_class < r_class))
    base = dot(jnp.where(ahead & (c_lon % chunk_lon == 0), 1.0, 0.0), size)
    place = rank + base[:, :lat_local]
    slot = jnp.zeros((lon_local, lat_local), jnp.float32)
    for n in range(TOP):
        slot = slot + masks[n] * place[n * lon_local : (n + 1) * lon_local]
    slot = slot.astype(jnp.int32)
    high, low = slot // LANES, slot % LANES
    highs = column_ref.shape[0]
    high_index = lax.broadcasted_iota(jnp.int32, (highs, lat_local), 0)
    low_index = lax.broadcasted_iota(jnp.int32, (LANES, lat_local), 0)
    lat = lax.broadcasted_iota(jnp.int32, (highs, lat_local), 1).astype(jnp.float32)
    found = jnp.zeros((highs, LANES), jnp.float32)
    number = jnp.zeros((highs, LANES), jnp.float32)
    for l in range(lon_local):
        at_high = jnp.where(high[l : l + 1] == high_index, 1.0, 0.0)
        at_low = jnp.where(low[l : l + 1] == low_index, 1.0, 0.0)
        both = jnp.concatenate([at_high, at_high * lat], axis=0)
        hit = lax.dot_general(both.astype(jnp.bfloat16), at_low.astype(jnp.bfloat16), (((1,), (1,)), ((), ())), preferred_element_type=jnp.float32)
        found = found + hit[:highs]
        number = number + hit[:highs] * float(l * lat_local) + hit[highs:]
    column = jnp.where(found > 0.5, number, float(lon_local * lat_local)).astype(jnp.int32)
    column_ref[...] = column
    row_ref[...] = column // 8 * 64 + column % 8
    row_index = lax.broadcasted_iota(jnp.int32, (rows, LANES), 0)
    lane = lax.broadcasted_iota(jnp.int32, (rows, LANES), 1)
    first = jnp.where(lane == row_index // lon_local, base, 0.0) + jnp.where(lane == TOP + row_index // lon_local, base + size, 0.0)
    bounds = []
    for k in range(chunks):
        bounds.append(jnp.sum(jnp.where(row_index % lon_local == k * chunk_lon, first, 0.0), axis=0, keepdims=True))
    bound_ref[...] = (jnp.concatenate(bounds, axis=0) * (1.0 / GROUP)).astype(jnp.int32)


def turn_quad(xs, odd, upper):
    def skew(xs):
        xs = [jnp.where(odd, xs[(i + 1) % 4], xs[i]) for i in range(4)]
        return [jnp.where(upper, xs[(i + 2) % 4], xs[i]) for i in range(4)]

    xs = skew(xs)
    xs = skew([xs[0]] + [pltpu.roll(xs[d], 32 * d, 1) for d in (1, 2, 3)])
    return [xs[-u % 4] for u in range(4)]


def cloud_kernel(column_ref, row_ref, bound_ref, state_ref, forcing_ref, courant_ref, out_ref, taken, given, ready, mid, done, power, in_sem, out_sem):
    chunks = bound_ref.shape[0]
    chunk_rows = state_ref.shape[1] // chunks
    levels = courant_ref.shape[1]

    def fetch(k):
        rows = pl.ds(pl.multiple_of(k * chunk_rows, 8), chunk_rows)
        return pltpu.make_async_copy(state_ref.at[:, rows], taken.at[:, rows], in_sem.at[k])

    def send(k):
        rows = pl.ds(pl.multiple_of(k * chunk_rows, 8), chunk_rows)
        return pltpu.make_async_copy(given.at[:, rows], out_ref.at[:, rows], out_sem.at[k])

    for k in range(chunks):
        fetch(k).start()

    rate = jnp.concatenate([courant_ref[...]] * (LANES // levels), axis=1)
    rate = jnp.broadcast_to(rate, (8, LANES))
    stay = 1.0 - rate
    for n in range(1, TOP + 1):
        for j in range(n + 1):
            value = jnp.full((8, LANES), math.comb(n, j) / 1.1, jnp.float32)
            for _ in range(j):
                value = value * rate
            for _ in range(n - j):
                value = value * stay
            power[n * (TOP + 1) + j] = value

    lane = lax.broadcasted_iota(jnp.int32, (8, LANES), 1)
    upper = lane >= 64
    odd = lane // 32 % 2 == 1
    power[0] = stay * ALPHA
    power[1] = rate * ALPHA

    def take(g):
        left = g * GROUP
        held = []
        for q in range(QUADS):
            dry, wet, push = [], [], []
            for c in range(4):
                row = row_ref[left + 4 * q + c]
                theta = taken[0, pl.ds(row, 8, stride=8), :]
                moist = taken[1, pl.ds(row, 8, stride=8), :]
                dry.append(theta + 0.5 * moist)
                wet.append(moist - 0.2 * theta)
                push.append(jnp.broadcast_to(forcing_ref[pl.ds(column_ref[left + 4 * q + c], 1), :], (8, LANES)))
            held += turn_quad(wet, odd, upper) + turn_quad(dry, odd, upper)
            held.append((0.2 * ALPHA) * jnp.where(upper, jnp.where(odd, push[3], push[2]), jnp.where(odd, push[1], push[0])))
        return held

    def keep(held):
        for i, x in enumerate(held):
            ready[i] = x

    gain = 0.725 / ALPHA
    floor = ALPHA * ALPHA * 0.01

    def drift(n):
        for q in range(QUADS):
            dry = [[ready[q * 9 + 4 + u] for u in range(4)]]
            dry.append([pltpu.roll(x, 1, 0) for x in dry[0]])
            if n > 4:
                dry.append([pltpu.roll(x, 2, 0) for x in dry[0]])
            shift = (n / (1.1 * 0.2 * ALPHA)) * ready[q * 9 + 8] - 0.5 / 1.1
            for u in range(4):
                total = shift
                for j in range(n + 1):
                    wraps = (j - u + 3) // 4 if j > u else 0
                    total = total + power[n * (TOP + 1) + j] * dry[wraps][(u - j) % 4]
                mid[q * 4 + u] = total

    def begin():
        wet = [[ready[q * 9 + u] for u in range(4)] for q in range(QUADS)]
        pull = [ready[q * 9 + 8] for q in range(QUADS)]
        return wet, pull

    def react(n, wet, pull):
        wet = list(wet)
        for s in range(n):
            keep_rate, move_rate = power[0], power[1]
            for q in range(QUADS):
                w = wet[q]
                less = pull[q] + ALPHA if s == 0 else pull[q]
                back = [pltpu.roll(w[3], 1, 0), w[0], w[1], w[2]]
                fresh = []
                for u in range(4):
                    e = keep_rate * w[u] + move_rate * back[u] - less
                    y = e * e + floor
                    fresh.append(gain * e - y * lax.rsqrt(y))
                wet[q] = fresh
        return wet

    def finish(wet):
        for q in range(QUADS):
            for u in range(4):
                theta = mid[q * 4 + u] - (0.5 / 1.1) * wet[q][u]
                done[q * 8 + u] = theta
                done[q * 8 + 4 + u] = wet[q][u] + 1.0 + 0.2 * theta

    def store(g):
        left = g * GROUP
        for q in range(QUADS):
            for field in range(2):
                turned = turn_quad([done[q * 8 + 4 * field + u] for u in range(4)], odd, upper)
                for c in range(4):
                    row = row_ref[left + 4 * q + c]
                    given[field, pl.ds(row, 8, stride=8), :] = turned[c]

    fetch(0).wait()
    keep(take(jnp.int32(0)))
    nothing = column_ref.shape[0] // GROUP - 1

    def chunk(k, last):
        @pl.when(k + 1 < chunks)
        def _():
            fetch(jnp.minimum(k + 1, chunks - 1)).wait()

        for n in range(1, TOP + 1):
            start, stop = bound_ref[k, n - 1], bound_ref[k, TOP + n - 1]

            def body(g, last, n=n):
                held = take(g + 1)
                wet, pull = begin()
                drift(n)
                keep(held)
                store(last)
                finish(react(n, wet, pull))
                return g

            last = lax.fori_loop(start, stop, body, last)

            @pl.when((k > 0) & (start == bound_ref[k, 0]) & (stop > start))
            def _():
                send(jnp.maximum(k - 1, 0)).start()

        return last

    last = lax.fori_loop(0, chunks, chunk, jnp.int32(nothing))
    store(last)
    send(chunks - 1).start()
    for k in range(chunks):
        send(k).wait()


def shards(cloud_state, counts, courant, truncation):
    lon_devices = lax.axis_size("lon")
    fields, lon_local, lat_local, cells = cloud_state.shape
    levels = courant.shape[0]
    total_modes = truncation.shape[0]
    pieces = cells // LANES
    columns = lon_local * lat_local
    chunks = 4
    slots = columns + chunks * TOP * (GROUP - 1) + 2 * GROUP
    highs = -(-slots // (8 * LANES)) * 8
    vmem = pl.BlockSpec(memory_space=pltpu.VMEM)
    smem = pl.BlockSpec(memory_space=pltpu.SMEM)
    column, row, bound = pl.pallas_call(
        order_kernel,
        in_specs=[vmem],
        out_specs=[vmem, vmem, vmem],
        out_shape=[
            jax.ShapeDtypeStruct((highs, LANES), jnp.int32),
            jax.ShapeDtypeStruct((highs, LANES), jnp.int32),
            jax.ShapeDtypeStruct((chunks, LANES), jnp.int32),
        ],
        name="order",
    )(counts)
    heating = jnp.mean(cloud_state[0], axis=2)
    held = gather_heating(heating, lon_devices)
    where = jnp.stack([lax.axis_index("lon"), lax.axis_index("lat")]).astype(jnp.int32)
    forcing = pl.pallas_call(
        spectral_kernel,
        in_specs=[smem, vmem, vmem, vmem],
        out_specs=vmem,
        out_shape=jax.ShapeDtypeStruct((columns + 8, LANES), jnp.float32),
        scratch_shapes=[
            pltpu.VMEM((NN, lat_local, LANES), jnp.float32),
            pltpu.VMEM((2, NN, 8, LANES), jnp.float32),
            pltpu.VMEM((1, LANES), jnp.int32),
        ],
        compiler_params=pltpu.CompilerParams(vmem_limit_bytes=48 << 20),
        name="spectral",
    )(where, held, truncation[None], courant[None])
    tiles = cloud_state.reshape(fields, lon_local, lat_local // 8, 8, pieces, LANES)
    tiles = tiles.transpose(0, 1, 2, 4, 3, 5).reshape(fields, columns * pieces, LANES)
    held_rows = columns * pieces + 8 * pieces
    out = pl.pallas_call(
        cloud_kernel,
        in_specs=[smem, smem, smem, pl.BlockSpec(memory_space=pl.ANY), vmem, vmem],
        out_specs=pl.BlockSpec(memory_space=pl.ANY),
        out_shape=jax.ShapeDtypeStruct(tiles.shape, jnp.float32),
        scratch_shapes=[
            pltpu.VMEM((fields, held_rows, LANES), jnp.float32),
            pltpu.VMEM((fields, held_rows, LANES), jnp.float32),
            pltpu.VMEM((QUADS * 9, 8, LANES), jnp.float32),
            pltpu.VMEM((QUADS * 4, 8, LANES), jnp.float32),
            pltpu.VMEM((QUADS * 8, 8, LANES), jnp.float32),
            pltpu.VMEM(((TOP + 1) ** 2, 8, LANES), jnp.float32),
            pltpu.SemaphoreType.DMA((chunks,)),
            pltpu.SemaphoreType.DMA((chunks,)),
        ],
        compiler_params=pltpu.CompilerParams(vmem_limit_bytes=60 << 20),
        name="clouds",
    )(column.reshape(-1), row.reshape(-1), bound, tiles, forcing, courant[None])
    out = out.reshape(fields, lon_local, lat_local // 8, pieces, 8, LANES)
    return out.transpose(0, 1, 2, 4, 3, 5).reshape(cloud_state.shape)


def solution(mesh):
    return jax.shard_map(
        shards,
        mesh=mesh,
        in_specs=(P("grp", "lon", "lat", None), P(("grp", "lon"), "lat"), P(), P()),
        out_specs=P("grp", "lon", "lat", None),
        check_vma=False,
    )
```

```python
import functools
import math

import jax
import jax.numpy as jnp
from jax import lax
from jax.experimental import pallas as pl
from jax.experimental.pallas import tpu as pltpu
from jax.sharding import PartitionSpec as P

NN = 96
couple_gain = 8.0
LANES = 128
HIGH = lax.Precision.HIGHEST
ALPHA = 0.275
GROUP = 16
QUADS = GROUP // 4
TOP = 8


def heating_kernel(state_ref, out_ref, held, sem):
    lon_local, lat_local, cells = held.shape
    lons = 4

    def fetch(k):
        return pltpu.make_async_copy(state_ref.at[0, pl.ds(k * lons, lons)], held.at[pl.ds(k * lons, lons)], sem.at[k])

    for k in range(lon_local // lons):
        fetch(k).start()
    ones = jnp.ones((8, LANES), jnp.float32)
    rows = lons * lat_local // LANES
    for k in range(lon_local // lons):
        fetch(k).wait()
        sums = []
        for l in range(k * lons, (k + 1) * lons):
            total = held[l, :, 0:LANES]
            for v in range(1, cells // LANES):
                total = total + held[l, :, v * LANES : (v + 1) * LANES]
            sums.append(total)
        means = contract(ones, jnp.concatenate(sums, axis=0), ((1,), (1,))) * (1.0 / cells)
        for r in range(rows):
            out_ref[k * rows + r : k * rows + r + 1, :] = means[0:1, r * LANES : (r + 1) * LANES]


def gather_heating(held, lon_devices):
    step = lon_devices // 2
    while step >= 1:
        pairs = [(i, i ^ step) for i in range(lon_devices)]
        with jax.named_scope(f"hop{step}"):
            moved = lax.ppermute(held, "lon", pairs)
        held = jnp.concatenate([held, moved], 0)
        step //= 2
    with jax.named_scope("hop0"):
        return held, lax.ppermute(held, "lat", [(0, 1), (1, 0)])


def contract(a, b, dims):
    return lax.dot_general(a, b, (dims, ((), ())), precision=HIGH, preferred_element_type=jnp.float32)


def tables_kernel(where_ref, trunc_ref, courant_ref, waves_ref, table_ref, rows_ref, *, lon_devices, lon_local):
    total_modes = trunc_ref.shape[1]
    levels = courant_ref.shape[1]
    lat_local = table_ref.shape[1]
    lon_index, lat_index = where_ref[0], where_ref[1]
    total_lon = lon_devices * lon_local
    total_lat = 2 * lat_local
    modes = lax.broadcasted_iota(jnp.int32, (1, LANES), 1)
    modes_f = modes.astype(jnp.float32)

    rows_ref[...] = jnp.full((8, LANES), -1.0, jnp.float32)
    rows_ref[0:1, :] = jnp.concatenate([courant_ref[...]] * (LANES // levels), axis=1)
    level = (modes % levels).astype(jnp.float32)
    rows_ref[1:2, :] = couple_gain * jnp.sin(jnp.pi * (level + 0.5) / levels)
    rows_ref[2:3, :total_modes] = trunc_ref[...].astype(jnp.float32)

    pack = waves_ref.shape[0]
    packed = waves_ref.shape[1]
    own = lon_local // pack
    row = lax.broadcasted_iota(jnp.int32, (packed, LANES), 0)
    lane = lax.broadcasted_iota(jnp.int32, (packed, LANES), 1)
    slot = row // own
    source = lon_index
    bit, step = 1, lon_devices // 2
    while step >= 1:
        source = source ^ jnp.where((slot & bit) != 0, step, 0)
        bit, step = bit * 2, step // 2
    carried = (lane < total_modes).astype(jnp.float32)
    for b in range(pack):
        phase = (source * lon_local + row % own * pack + b) * lane % total_lon
        angle = phase.astype(jnp.float32) * (2.0 * jnp.pi / total_lon)
        waves_ref[b, :, :LANES] = jnp.cos(angle) * carried
        waves_ref[b, :, LANES:] = jnp.sin(angle) * carried

    rows = (lat_index * lat_local + lax.broadcasted_iota(jnp.int32, (lat_local, 1), 0)).astype(jnp.float32)
    latitude = -0.5 * jnp.pi + jnp.pi * (rows + 0.5) / total_lat
    sin_lat = jnp.broadcast_to(jnp.sin(latitude), (lat_local, LANES))
    cos_lat = jnp.cos(latitude)
    ladder = (lax.broadcasted_iota(jnp.int32, (NN, LANES), 0) + 1).astype(jnp.float32)
    gains = 0.5 * jnp.log((2.0 * ladder + 1.0) / (2.0 * ladder))
    log_start = 0.5 * jnp.log(jnp.float32(0.5)) + jnp.sum(
        jnp.where(ladder <= modes_f, gains, 0.0), axis=0, keepdims=True
    )
    diagonal = jnp.exp(log_start + modes_f * jnp.log(cos_lat))
    degree = lax.broadcasted_iota(jnp.int32, (NN, LANES), 0).astype(jnp.float32)

    def factor_of(degree_f):
        higher = degree_f > modes_f
        numerator = jnp.maximum(4.0 * degree_f * degree_f - 1.0, 1.0)
        denominator = jnp.where(higher, degree_f * degree_f - modes_f * modes_f, 1.0)
        return higher, jnp.sqrt(numerator / denominator)

    higher, factor = factor_of(degree)
    factor = jnp.where(higher, factor, 0.0)
    below, lower_factor = factor_of(degree - 1.0)
    ratio = jnp.where(below, factor / lower_factor, 0.0)
    previous = jnp.zeros((lat_local, LANES), jnp.float32)
    earlier = jnp.zeros((lat_local, LANES), jnp.float32)
    for n in range(NN):
        raised = factor[n : n + 1] * (sin_lat * previous) - ratio[n : n + 1] * earlier
        current = jnp.where(modes == n, diagonal, raised)
        table_ref[n] = current
        previous, earlier = current, previous


def spectral_forcing(where_ref, mine_ref, others_ref, rows_ref, waves_ref, table_ref, out_ref, partial):
    pack, packed = waves_ref.shape[:2]
    lat_local = table_ref.shape[1]
    own = (out_ref.shape[0] - 8) // lat_local // pack
    lat_index = where_ref[1]
    total_lon = packed * pack
    total_lat = 2 * lat_local
    modes = lax.broadcasted_iota(jnp.int32, (1, LANES), 1)
    rows = (lat_index * lat_local + lax.broadcasted_iota(jnp.int32, (lat_local, 1), 0)).astype(jnp.float32)
    latitude = -0.5 * jnp.pi + jnp.pi * (rows + 0.5) / total_lat
    weight = jnp.pi * jnp.cos(latitude) / total_lat / total_lon

    def transform(ref):
        held = ref[...]
        total = 0.0
        for b in range(pack):
            total = total + contract(held, waves_ref[b], ((0,), (0,)))[b * lat_local : (b + 1) * lat_local]
        return total

    mine = transform(mine_ref)
    others = transform(others_ref)
    r = lax.broadcasted_iota(jnp.int32, (lat_local, lat_local), 0)
    c = lax.broadcasted_iota(jnp.int32, (lat_local, lat_local), 1)
    flip = (r + c == lat_local - 1).astype(jnp.float32)
    others = contract(flip, others, ((1,), (0,)))
    same = (mine + others) * weight
    diff = (mine - others) * weight
    lane2 = lax.broadcasted_iota(jnp.int32, (1, 2 * LANES), 1)
    even_mode = lane2 % 2 == 0
    folded = [jnp.where(even_mode, same, diff), jnp.where(even_mode, diff, same)]
    for parity in range(2):
        for part in range(2):
            values = folded[parity][:, part * LANES : (part + 1) * LANES]
            for n in range(parity, NN, 2):
                terms = table_ref[n] * values
                partial[part, n] = sum(terms[8 * i : 8 * i + 8] for i in range(lat_local // 8))

    degree_i = lax.broadcasted_iota(jnp.int32, (NN, LANES), 0)
    keep = (degree_i >= modes) & (degree_i.astype(jnp.float32) <= rows_ref[2:3, :])
    scale = jnp.where(modes == 0, 1.0, 2.0)
    filtered = []
    for part in range(2):
        spectrum = jnp.where(keep, jnp.sum(partial[part], axis=1) * scale, 0.0)
        total = jnp.zeros((lat_local, LANES), jnp.float32)
        for n in range(NN):
            total = total + table_ref[n] * spectrum[n : n + 1]
        filtered.append(total)
    filtered = jnp.concatenate(filtered, axis=1)
    forcing = [contract(filtered, waves_ref[b, :own], ((1,), (1,))) for b in range(pack)]
    profile = rows_ref[1:2, :]
    for l in range(own * pack):
        out_ref[l * lat_local : (l + 1) * lat_local] = forcing[l % pack][:, l // pack : l // pack + 1] * profile


def order_kernel(counts_ref, column_ref, row_ref, bound_ref):
    lon_local, lat_local = counts_ref.shape
    chunks = bound_ref.shape[0]
    chunk_lon = lon_local // chunks
    counts = counts_ref[...]
    rows = TOP * lon_local
    masks = [jnp.where(counts == n + 1, 1.0, 0.0) for n in range(TOP)]
    mask = jnp.concatenate(masks, axis=0).astype(jnp.bfloat16)

    def dot(a, b):
        return lax.dot_general(a.astype(jnp.bfloat16), b.astype(jnp.bfloat16), (((1,), (0,)), ((), ())), preferred_element_type=jnp.float32)

    r = lax.broadcasted_iota(jnp.int32, (lat_local, lat_local), 0)
    c = lax.broadcasted_iota(jnp.int32, (lat_local, lat_local), 1)
    before = dot(mask, jnp.where(r < c, 1.0, 0.0))
    total = dot(mask, jnp.ones((lat_local, LANES), jnp.float32))
    r = lax.broadcasted_iota(jnp.int32, (rows, rows), 0)
    c = lax.broadcasted_iota(jnp.int32, (rows, rows), 1)
    r_class, r_lon, c_class, c_lon = r // lon_local, r % lon_local, c // lon_local, c % lon_local
    same_chunk = r_lon // chunk_lon == c_lon // chunk_lon
    same_class = (r_class == c_class) & same_chunk
    rank = before + dot(jnp.where(same_class & (c_lon < r_lon), 1.0, 0.0), total)[:, :lat_local]
    size = dot(jnp.where(same_class, 1.0, 0.0), total)
    size = jnp.floor((size + (GROUP - 1)) * (1.0 / GROUP)) * GROUP
    ahead = (c_lon // chunk_lon < r_lon // chunk_lon) | (same_chunk & (c_class < r_class))
    base = dot(jnp.where(ahead & (c_lon % chunk_lon == 0), 1.0, 0.0), size)
    place = rank + base[:, :lat_local]
    slot = jnp.zeros((lon_local, lat_local), jnp.float32)
    for n in range(TOP):
        slot = slot + masks[n] * place[n * lon_local : (n + 1) * lon_local]
    slot = slot.astype(jnp.int32)
    high, low = slot // LANES, slot % LANES
    highs = column_ref.shape[0]
    high_index = lax.broadcasted_iota(jnp.int32, (highs, lat_local), 0)
    low_index = lax.broadcasted_iota(jnp.int32, (LANES, lat_local), 0)
    lat = lax.broadcasted_iota(jnp.int32, (highs, lat_local), 1).astype(jnp.float32)
    found = jnp.zeros((highs, LANES), jnp.float32)
    number = jnp.zeros((highs, LANES), jnp.float32)
    for l in range(lon_local):
        at_high = jnp.where(high[l : l + 1] == high_index, 1.0, 0.0)
        at_low = jnp.where(low[l : l + 1] == low_index, 1.0, 0.0)
        both = jnp.concatenate([at_high, at_high * lat], axis=0)
        hit = lax.dot_general(both.astype(jnp.bfloat16), at_low.astype(jnp.bfloat16), (((1,), (1,)), ((), ())), preferred_element_type=jnp.float32)
        found = found + hit[:highs]
        number = number + hit[:highs] * float(l * lat_local) + hit[highs:]
    column = jnp.where(found > 0.5, number, float(lon_local * lat_local)).astype(jnp.int32)
    column_ref[...] = column
    row_ref[...] = column // 8 * 64 + column % 8
    row_index = lax.broadcasted_iota(jnp.int32, (rows, LANES), 0)
    lane = lax.broadcasted_iota(jnp.int32, (rows, LANES), 1)
    first = jnp.where(lane == row_index // lon_local, base, 0.0) + jnp.where(lane == TOP + row_index // lon_local, base + size, 0.0)
    bounds = []
    for k in range(chunks):
        bounds.append(jnp.sum(jnp.where(row_index % lon_local == k * chunk_lon, first, 0.0), axis=0, keepdims=True))
    bound_ref[...] = (jnp.concatenate(bounds, axis=0) * (1.0 / GROUP)).astype(jnp.int32)


def skew(xs, odd, upper):
    xs = [jnp.where(odd, xs[(i + 1) % 4], xs[i]) for i in range(4)]
    return [jnp.where(upper, xs[(i + 2) % 4], xs[i]) for i in range(4)]


def cloud_kernel(column_ref, row_ref, bound_ref, where_ref, state_ref, mine_ref, others_ref, rows_ref, waves_ref, table_ref, out_ref, taken, given, forcing_ref, partial, stage, ready, mid, done, power, in_sem, out_sem):
    chunks = bound_ref.shape[0]
    chunk_rows = state_ref.shape[1] // chunks

    def fetch(k):
        rows = pl.ds(pl.multiple_of(k * chunk_rows, 8), chunk_rows)
        return pltpu.make_async_copy(state_ref.at[:, rows], taken.at[:, rows], in_sem.at[k])

    def send(k):
        rows = pl.ds(pl.multiple_of(k * chunk_rows, 8), chunk_rows)
        return pltpu.make_async_copy(given.at[:, rows], out_ref.at[:, rows], out_sem.at[k])

    for k in range(chunks):
        fetch(k).start()
    spectral_forcing(where_ref, mine_ref, others_ref, rows_ref, waves_ref, table_ref, forcing_ref, partial)

    rate = jnp.broadcast_to(rows_ref[0:1, :], (8, LANES))
    stay = 1.0 - rate
    for n in range(1, TOP + 1):
        for j in range(n + 1):
            value = jnp.full((8, LANES), math.comb(n, j) / 1.1, jnp.float32)
            for _ in range(j):
                value = value * rate
            for _ in range(n - j):
                value = value * stay
            power[n * (TOP + 1) + j] = value

    lane = lax.broadcasted_iota(jnp.int32, (8, LANES), 1)
    upper = lane >= 64
    odd = lane // 32 % 2 == 1
    lanes = [lane // 32 == g for g in range(4)]
    power[0] = stay * ALPHA
    power[1] = rate * ALPHA

    def rotate(xs):
        return [xs[0]] + [pltpu.roll(xs[d], 32 * d, 1) for d in (1, 2, 3)]

    def take(g):
        left = g * GROUP
        held = []
        for q in range(QUADS):
            push = []
            for c in range(4):
                row = row_ref[left + 4 * q + c]
                theta = taken[0, pl.ds(row, 8, stride=8), :]
                moist = taken[1, pl.ds(row, 8, stride=8), :]
                held.append((moist - 0.2 * theta, theta + 0.5 * moist))
                push.append(jnp.broadcast_to(forcing_ref[pl.ds(column_ref[left + 4 * q + c], 1), :], (8, LANES)))
            held.append((0.2 * ALPHA) * jnp.where(upper, jnp.where(odd, push[3], push[2]), jnp.where(odd, push[1], push[0])))
        return held

    def put(held):
        for q in range(QUADS):
            quad = held[5 * q : 5 * q + 4]
            for d, x in enumerate(skew([x for x, _ in quad], odd, upper) + skew([x for _, x in quad], odd, upper)):
                stage[q * 9 + d] = x
            stage[q * 9 + 8] = held[5 * q + 4]

    def turn():
        return [
            (rotate([stage[q * 9 + d] for d in range(4)]), rotate([stage[q * 9 + 4 + d] for d in range(4)]), stage[q * 9 + 8])
            for q in range(QUADS)
        ]

    def keep(rolled):
        for q, (wet, dry, pull) in enumerate(rolled):
            wet, dry = skew(wet, odd, upper), skew(dry, odd, upper)
            for u in range(4):
                ready[q * 9 + u] = wet[-u % 4]
                ready[q * 9 + 4 + u] = dry[-u % 4]
            ready[q * 9 + 8] = pull

    gain = 0.725 / ALPHA
    floor = ALPHA * ALPHA * 0.01

    def drift(n):
        for q in range(QUADS):
            dry = [[ready[q * 9 + 4 + u] for u in range(4)]]
            dry.append([pltpu.roll(x, 1, 0) for x in dry[0]])
            if n > 4:
                dry.append([pltpu.roll(x, 2, 0) for x in dry[0]])
            shift = (n / (1.1 * 0.2 * ALPHA)) * ready[q * 9 + 8] - 0.5 / 1.1
            for u in range(4):
                total = shift
                for j in range(n + 1):
                    wraps = (j - u + 3) // 4 if j > u else 0
                    total = total + power[n * (TOP + 1) + j] * dry[wraps][(u - j) % 4]
                mid[q * 4 + u] = total

    def begin():
        wet = [[ready[q * 9 + u] for u in range(4)] for q in range(QUADS)]
        pull = [ready[q * 9 + 8] for q in range(QUADS)]
        return wet, pull

    def react(n, wet, pull):
        wet = list(wet)
        for s in range(n):
            keep_rate, move_rate = power[0], power[1]
            for q in range(QUADS):
                w = wet[q]
                less = pull[q] + ALPHA if s == 0 else pull[q]
                back = [pltpu.roll(w[3], 1, 0), w[0], w[1], w[2]]
                fresh = []
                for u in range(4):
                    e = keep_rate * w[u] + move_rate * back[u] - less
                    y = e * e + floor
                    fresh.append(gain * e - y * lax.rsqrt(y))
                wet[q] = fresh
        return wet

    def finish(wet):
        for q in range(QUADS):
            theta = [mid[q * 4 + u] - (0.5 / 1.1) * wet[q][u] for u in range(4)]
            moist = [wet[q][u] + 1.0 + 0.2 * theta[u] for u in range(4)]
            for d, x in enumerate(skew(theta, odd, upper) + skew(moist, odd, upper)):
                done[q * 8 + d] = x

    def store(g):
        left = g * GROUP
        for q in range(QUADS):
            for field in range(2):
                xs = skew(rotate([done[q * 8 + 4 * field + d] for d in range(4)]), odd, upper)
                for c in range(4):
                    given[field, pl.ds(row_ref[left + 4 * q + c], 8, stride=8), :] = xs[-c % 4]

    fetch(0).wait()
    put(take(jnp.int32(0)))
    keep(turn())
    put(take(jnp.int32(1)))
    nothing = column_ref.shape[0] // GROUP - 1

    def chunk(k, last):
        @pl.when(k + 1 < chunks)
        def _():
            fetch(jnp.minimum(k + 1, chunks - 1)).wait()

        for n in range(1, TOP + 1):
            start, stop = bound_ref[k, n - 1], bound_ref[k, TOP + n - 1]

            def body(g, last, n=n):
                held = take(g + 2)
                rolled = turn()
                wet, pull = begin()
                drift(n)
                put(held)
                keep(rolled)
                store(last)
                finish(react(n, wet, pull))
                return g

            last = lax.fori_loop(start, stop, body, last)

            @pl.when((k > 0) & (start == bound_ref[k, 0]) & (stop > start))
            def _():
                send(jnp.maximum(k - 1, 0)).start()

        return last

    last = lax.fori_loop(0, chunks, chunk, jnp.int32(nothing))
    store(last)
    send(chunks - 1).start()
    for k in range(chunks):
        send(k).wait()


def shards(cloud_state, counts, courant, truncation):
    lon_devices = lax.axis_size("lon")
    fields, lon_local, lat_local, cells = cloud_state.shape
    pieces = cells // LANES
    columns = lon_local * lat_local
    chunks = 4
    slots = columns + chunks * TOP * (GROUP - 1) + 2 * GROUP
    highs = -(-slots // (8 * LANES)) * 8
    vmem = pl.BlockSpec(memory_space=pltpu.VMEM)
    smem = pl.BlockSpec(memory_space=pltpu.SMEM)
    column, row, bound = pl.pallas_call(
        order_kernel,
        in_specs=[vmem],
        out_specs=[vmem, vmem, vmem],
        out_shape=[
            jax.ShapeDtypeStruct((highs, LANES), jnp.int32),
            jax.ShapeDtypeStruct((highs, LANES), jnp.int32),
            jax.ShapeDtypeStruct((chunks, LANES), jnp.int32),
        ],
        compiler_params=pltpu.CompilerParams(vmem_limit_bytes=16 << 20),
        name="order",
    )(counts)
    pack = LANES // lat_local
    heating = pl.pallas_call(
        heating_kernel,
        in_specs=[pl.BlockSpec(memory_space=pl.ANY)],
        out_specs=vmem,
        out_shape=jax.ShapeDtypeStruct((lon_local // pack, LANES), jnp.float32),
        scratch_shapes=[
            pltpu.VMEM((lon_local, lat_local, cells), jnp.float32),
            pltpu.SemaphoreType.DMA((lon_local // 4,)),
        ],
        compiler_params=pltpu.CompilerParams(vmem_limit_bytes=50 << 20),
        name="heating",
    )(cloud_state)
    where = jnp.stack([lax.axis_index("lon"), lax.axis_index("lat")]).astype(jnp.int32)
    waves, table, rows = pl.pallas_call(
        functools.partial(tables_kernel, lon_devices=lon_devices, lon_local=lon_local),
        in_specs=[smem, vmem, vmem],
        out_specs=[vmem, vmem, vmem],
        out_shape=[
            jax.ShapeDtypeStruct((pack, lon_devices * lon_local // pack, 2 * LANES), jnp.float32),
            jax.ShapeDtypeStruct((NN, lat_local, LANES), jnp.float32),
            jax.ShapeDtypeStruct((8, LANES), jnp.float32),
        ],
        compiler_params=pltpu.CompilerParams(vmem_limit_bytes=16 << 20),
        name="tables",
    )(where, truncation[None], courant[None])
    mine, others = gather_heating(heating, lon_devices)
    tiles = cloud_state.reshape(fields, lon_local, lat_local // 8, 8, pieces, LANES)
    tiles = tiles.transpose(0, 1, 2, 4, 3, 5).reshape(fields, columns * pieces, LANES)
    held_rows = columns * pieces + 8 * pieces
    out = pl.pallas_call(
        cloud_kernel,
        in_specs=[smem, smem, smem, smem, pl.BlockSpec(memory_space=pl.ANY)] + [vmem] * 5,
        out_specs=pl.BlockSpec(memory_space=pl.ANY),
        out_shape=jax.ShapeDtypeStruct(tiles.shape, jnp.float32),
        scratch_shapes=[
            pltpu.VMEM((fields, held_rows, LANES), jnp.float32),
            pltpu.VMEM((fields, held_rows, LANES), jnp.float32),
            pltpu.VMEM((columns + 8, LANES), jnp.float32),
            pltpu.VMEM((2, NN, 8, LANES), jnp.float32),
            pltpu.VMEM((QUADS * 9, 8, LANES), jnp.float32),
            pltpu.VMEM((QUADS * 9, 8, LANES), jnp.float32),
            pltpu.VMEM((QUADS * 4, 8, LANES), jnp.float32),
            pltpu.VMEM((QUADS * 8, 8, LANES), jnp.float32),
            pltpu.VMEM(((TOP + 1) ** 2, 8, LANES), jnp.float32),
            pltpu.SemaphoreType.DMA((chunks,)),
            pltpu.SemaphoreType.DMA((chunks,)),
        ],
        compiler_params=pltpu.CompilerParams(vmem_limit_bytes=44 << 20),
        name="clouds",
    )(column.reshape(-1), row.reshape(-1), bound, where, tiles, mine, others, rows, waves, table)
    out = out.reshape(fields, lon_local, lat_local // 8, pieces, 8, LANES)
    return out.transpose(0, 1, 2, 4, 3, 5).reshape(cloud_state.shape)


def solution(mesh):
    return jax.shard_map(
        shards,
        mesh=mesh,
        in_specs=(P("grp", "lon", "lat", None), P(("grp", "lon"), "lat"), P(), P()),
        out_specs=P("grp", "lon", "lat", None),
        check_vma=False,
    )
```

```python
import functools
import math

import jax
import jax.numpy as jnp
from jax import lax
from jax.experimental import pallas as pl
from jax.experimental.pallas import tpu as pltpu
from jax.sharding import PartitionSpec as P


NN = 96
couple_gain = 8.0
LANES = 128
ALPHA = 0.275
GROUP = 16
QUADS = GROUP // 4
TOP = 8


def heating_kernel(state_ref, out_ref, held, sem):
    lon_local, lat_local, cells = held.shape
    lons = 4

    def fetch(k):
        return pltpu.make_async_copy(state_ref.at[0, pl.ds(k * lons, lons)], held.at[pl.ds(k * lons, lons)], sem.at[k])

    for k in range(lon_local // lons):
        fetch(k).start()
    ones = jnp.ones((8, LANES), jnp.float32)
    rows = lons * lat_local // LANES
    for k in range(lon_local // lons):
        fetch(k).wait()
        sums = []
        for l in range(k * lons, (k + 1) * lons):
            total = held[l, :, 0:LANES]
            for v in range(1, cells // LANES):
                total = total + held[l, :, v * LANES : (v + 1) * LANES]
            sums.append(total)
        means = contract(ones, jnp.concatenate(sums, axis=0), ((1,), (1,))) * (1.0 / cells)
        for r in range(rows):
            out_ref[k * rows + r : k * rows + r + 1, :] = means[0:1, r * LANES : (r + 1) * LANES]


def gather_heating(held, lon_devices):
    step = lon_devices // 2
    while step >= 1:
        pairs = [(i, i ^ step) for i in range(lon_devices)]
        moved = lax.ppermute(held, "lon", pairs)
        held = jnp.concatenate([held, moved], 0)
        step //= 2
    return held, lax.ppermute(held, "lat", [(0, 1), (1, 0)])


def halves(x):
    high = x.astype(jnp.bfloat16)
    return high, (x - high.astype(jnp.float32)).astype(jnp.bfloat16)


def contract(a, b, dims):
    a_high, a_low = halves(a)
    b_high, b_low = halves(b)

    def dot(a, b):
        return lax.dot_general(a, b, (dims, ((), ())), preferred_element_type=jnp.float32)

    return dot(a_high, b_high) + (dot(a_low, b_high) + dot(a_high, b_low))


def tables_kernel(where_ref, trunc_ref, courant_ref, waves_ref, table_ref, rows_ref, *, lon_devices, lon_local):
    total_modes = trunc_ref.shape[1]
    levels = courant_ref.shape[1]
    lat_local = table_ref.shape[1]
    lon_index, lat_index = where_ref[0], where_ref[1]
    total_lon = lon_devices * lon_local
    total_lat = 2 * lat_local
    modes = lax.broadcasted_iota(jnp.int32, (1, LANES), 1)
    modes_f = modes.astype(jnp.float32)

    rows_ref[...] = jnp.full((8, LANES), -1.0, jnp.float32)
    rows_ref[0:1, :] = jnp.concatenate([courant_ref[...]] * (LANES // levels), axis=1)
    level = (modes % levels).astype(jnp.float32)
    rows_ref[1:2, :] = couple_gain * jnp.sin(jnp.pi * (level + 0.5) / levels)
    rows_ref[2:3, :total_modes] = trunc_ref[...].astype(jnp.float32)

    pack = waves_ref.shape[0]
    packed = waves_ref.shape[1]
    own = lon_local // pack
    row = lax.broadcasted_iota(jnp.int32, (packed, LANES), 0)
    lane = lax.broadcasted_iota(jnp.int32, (packed, LANES), 1)
    slot = row // own
    source = lon_index
    bit, step = 1, lon_devices // 2
    while step >= 1:
        source = source ^ jnp.where((slot & bit) != 0, step, 0)
        bit, step = bit * 2, step // 2
    carried = (lane < total_modes).astype(jnp.float32)
    for b in range(pack):
        phase = (source * lon_local + row % own * pack + b) * lane % total_lon
        angle = phase.astype(jnp.float32) * (2.0 * jnp.pi / total_lon)
        waves_ref[b, :, :LANES] = jnp.cos(angle) * carried
        waves_ref[b, :, LANES:] = jnp.sin(angle) * carried

    rows = (lat_index * lat_local + lax.broadcasted_iota(jnp.int32, (lat_local, 1), 0)).astype(jnp.float32)
    latitude = -0.5 * jnp.pi + jnp.pi * (rows + 0.5) / total_lat
    sin_lat = jnp.broadcast_to(jnp.sin(latitude), (lat_local, LANES))
    cos_lat = jnp.cos(latitude)
    ladder = (lax.broadcasted_iota(jnp.int32, (NN, LANES), 0) + 1).astype(jnp.float32)
    gains = 0.5 * jnp.log((2.0 * ladder + 1.0) / (2.0 * ladder))
    log_start = 0.5 * jnp.log(jnp.float32(0.5)) + jnp.sum(
        jnp.where(ladder <= modes_f, gains, 0.0), axis=0, keepdims=True
    )
    diagonal = jnp.exp(log_start + modes_f * jnp.log(cos_lat))
    degree = lax.broadcasted_iota(jnp.int32, (NN, LANES), 0).astype(jnp.float32)

    def factor_of(degree_f):
        higher = degree_f > modes_f
        numerator = jnp.maximum(4.0 * degree_f * degree_f - 1.0, 1.0)
        denominator = jnp.where(higher, degree_f * degree_f - modes_f * modes_f, 1.0)
        return higher, jnp.sqrt(numerator / denominator)

    higher, factor = factor_of(degree)
    factor = jnp.where(higher, factor, 0.0)
    below, lower_factor = factor_of(degree - 1.0)
    ratio = jnp.where(below, factor / lower_factor, 0.0)
    previous = jnp.zeros((lat_local, LANES), jnp.float32)
    earlier = jnp.zeros((lat_local, LANES), jnp.float32)
    for n in range(NN):
        raised = factor[n : n + 1] * (sin_lat * previous) - ratio[n : n + 1] * earlier
        current = jnp.where(modes == n, diagonal, raised)
        table_ref[n] = current
        previous, earlier = current, previous


def spectral_forcing(where_ref, mine_ref, others_ref, rows_ref, waves_ref, table_ref, out_ref, partial):
    pack, packed = waves_ref.shape[:2]
    lat_local = table_ref.shape[1]
    own = (out_ref.shape[0] - 8) // lat_local // pack
    lat_index = where_ref[1]
    total_lon = packed * pack
    total_lat = 2 * lat_local
    modes = lax.broadcasted_iota(jnp.int32, (1, LANES), 1)
    rows = (lat_index * lat_local + lax.broadcasted_iota(jnp.int32, (lat_local, 1), 0)).astype(jnp.float32)
    latitude = -0.5 * jnp.pi + jnp.pi * (rows + 0.5) / total_lat
    weight = jnp.pi * jnp.cos(latitude) / total_lat / total_lon

    def transform(ref):
        held = ref[...]
        total = 0.0
        for b in range(pack):
            total = total + contract(held, waves_ref[b], ((0,), (0,)))[b * lat_local : (b + 1) * lat_local]
        return total

    mine = transform(mine_ref)
    others = transform(others_ref)
    r = lax.broadcasted_iota(jnp.int32, (lat_local, lat_local), 0)
    c = lax.broadcasted_iota(jnp.int32, (lat_local, lat_local), 1)
    flip = (r + c == lat_local - 1).astype(jnp.float32)
    others = contract(flip, others, ((1,), (0,)))
    same = (mine + others) * weight
    diff = (mine - others) * weight
    lane2 = lax.broadcasted_iota(jnp.int32, (1, 2 * LANES), 1)
    even_mode = lane2 % 2 == 0
    folded = [jnp.where(even_mode, same, diff), jnp.where(even_mode, diff, same)]
    for parity in range(2):
        for part in range(2):
            values = folded[parity][:, part * LANES : (part + 1) * LANES]
            for n in range(parity, NN, 2):
                terms = table_ref[n] * values
                partial[part, n] = sum(terms[8 * i : 8 * i + 8] for i in range(lat_local // 8))

    degree_i = lax.broadcasted_iota(jnp.int32, (NN, LANES), 0)
    keep = (degree_i >= modes) & (degree_i.astype(jnp.float32) <= rows_ref[2:3, :])
    scale = jnp.where(modes == 0, 1.0, 2.0)
    filtered = []
    for part in range(2):
        spectrum = jnp.where(keep, jnp.sum(partial[part], axis=1) * scale, 0.0)
        total = jnp.zeros((lat_local, LANES), jnp.float32)
        for n in range(NN):
            total = total + table_ref[n] * spectrum[n : n + 1]
        filtered.append(total)
    filtered = jnp.concatenate(filtered, axis=1)
    forcing = [contract(filtered, waves_ref[b, :own], ((1,), (1,))) for b in range(pack)]
    profile = rows_ref[1:2, :]
    for l in range(own * pack):
        out_ref[l * lat_local : (l + 1) * lat_local] = forcing[l % pack][:, l // pack : l // pack + 1] * profile


def chunk_ends(lon_local):
    return [lon_local * 15 // 32, lon_local * 27 // 32, lon_local]


def order_kernel(counts_ref, column_ref, row_ref, bound_ref):
    lon_local, lat_local = counts_ref.shape
    ends = chunk_ends(lon_local)
    counts = counts_ref[...]
    rows = TOP * lon_local
    masks = [jnp.where(counts == n + 1, 1.0, 0.0) for n in range(TOP)]
    mask = jnp.concatenate(masks, axis=0).astype(jnp.bfloat16)

    def dot(a, b):
        return lax.dot_general(a.astype(jnp.bfloat16), b.astype(jnp.bfloat16), (((1,), (0,)), ((), ())), preferred_element_type=jnp.float32)

    r = lax.broadcasted_iota(jnp.int32, (lat_local, lat_local), 0)
    c = lax.broadcasted_iota(jnp.int32, (lat_local, lat_local), 1)
    before = dot(mask, jnp.where(r < c, 1.0, 0.0))
    total = dot(mask, jnp.ones((lat_local, LANES), jnp.float32))
    r = lax.broadcasted_iota(jnp.int32, (rows, rows), 0)
    c = lax.broadcasted_iota(jnp.int32, (rows, rows), 1)
    r_class, r_lon, c_class, c_lon = r // lon_local, r % lon_local, c // lon_local, c % lon_local
    chunk_of = lambda lon: sum(jnp.where(lon >= end, 1, 0) for end in ends[:-1])
    opens = functools.reduce(jnp.logical_or, [c_lon == lon for lon in [0] + ends[:-1]])
    r_chunk, c_chunk = chunk_of(r_lon), chunk_of(c_lon)
    same_chunk = r_chunk == c_chunk
    same_class = (r_class == c_class) & same_chunk
    rank = before + dot(jnp.where(same_class & (c_lon < r_lon), 1.0, 0.0), total)[:, :lat_local]
    size = dot(jnp.where(same_class, 1.0, 0.0), total)
    size = jnp.floor((size + (GROUP - 1)) * (1.0 / GROUP)) * GROUP
    ahead = (c_chunk < r_chunk) | (same_chunk & (c_class < r_class))
    base = dot(jnp.where(ahead & opens, 1.0, 0.0), size)
    place = rank + base[:, :lat_local]
    slot = jnp.zeros((lon_local, lat_local), jnp.float32)
    for n in range(TOP):
        slot = slot + masks[n] * place[n * lon_local : (n + 1) * lon_local]
    slot = slot.astype(jnp.int32)
    high, low = slot // LANES, slot % LANES
    highs = column_ref.shape[0]
    high_index = lax.broadcasted_iota(jnp.int32, (highs, lat_local), 0)
    low_index = lax.broadcasted_iota(jnp.int32, (LANES, lat_local), 0)
    lat = lax.broadcasted_iota(jnp.int32, (highs, lat_local), 1).astype(jnp.float32)
    found = jnp.zeros((highs, LANES), jnp.float32)
    number = jnp.zeros((highs, LANES), jnp.float32)
    for l in range(lon_local):
        at_high = jnp.where(high[l : l + 1] == high_index, 1.0, 0.0)
        at_low = jnp.where(low[l : l + 1] == low_index, 1.0, 0.0)
        both = jnp.concatenate([at_high, at_high * lat], axis=0)
        hit = lax.dot_general(both.astype(jnp.bfloat16), at_low.astype(jnp.bfloat16), (((1,), (1,)), ((), ())), preferred_element_type=jnp.float32)
        found = found + hit[:highs]
        number = number + hit[:highs] * float(l * lat_local) + hit[highs:]
    column = jnp.where(found > 0.5, number, float(lon_local * lat_local)).astype(jnp.int32)
    column_ref[...] = column
    row_ref[...] = column // 8 * 64 + column % 8
    row_index = lax.broadcasted_iota(jnp.int32, (rows, LANES), 0)
    lane = lax.broadcasted_iota(jnp.int32, (rows, LANES), 1)
    first = jnp.where(lane == row_index // lon_local, base, 0.0) + jnp.where(lane == TOP + row_index // lon_local, base + size, 0.0)
    bounds = []
    for start in [0] + ends[:-1]:
        bounds.append(jnp.sum(jnp.where(row_index % lon_local == start, first, 0.0), axis=0, keepdims=True))
    bound_ref[...] = (jnp.concatenate(bounds, axis=0) * (1.0 / GROUP)).astype(jnp.int32)


def skew(xs, odd, upper):
    xs = [jnp.where(odd, xs[(i + 1) % 4], xs[i]) for i in range(4)]
    return [jnp.where(upper, xs[(i + 2) % 4], xs[i]) for i in range(4)]


def cloud_kernel(column_ref, row_ref, bound_ref, where_ref, state_ref, mine_ref, others_ref, rows_ref, waves_ref, table_ref, out_ref, taken, given, forcing_ref, partial, stage, ready, mid, done, power, in_sem, out_sem, *, lon_local):
    chunks = bound_ref.shape[0]
    lon_rows = state_ref.shape[1] // lon_local
    splits = [0] + chunk_ends(lon_local)

    def parts(k, count):
        cuts = [splits[k] + (splits[k + 1] - splits[k]) * i // count for i in range(count + 1)]
        return [pl.ds(a * lon_rows, (b - a) * lon_rows) for a, b in zip(cuts, cuts[1:])]

    def fetch(k):
        return [
            pltpu.make_async_copy(state_ref.at[:, rows], taken.at[:, rows], in_sem.at[k, i])
            for i, rows in enumerate(parts(k, in_sem.shape[1]))
        ]

    def send(k):
        return [
            pltpu.make_async_copy(given.at[:, rows], out_ref.at[:, rows], out_sem.at[k, i])
            for i, rows in enumerate(parts(k, out_sem.shape[1]))
        ]

    for k in range(chunks):
        for copy in fetch(k):
            copy.start()
    spectral_forcing(where_ref, mine_ref, others_ref, rows_ref, waves_ref, table_ref, forcing_ref, partial)

    rate = jnp.broadcast_to(rows_ref[0:1, :], (8, LANES))
    stay = 1.0 - rate
    for n in range(1, TOP + 1):
        for j in range(n + 1):
            value = jnp.full((8, LANES), math.comb(n, j) / 1.1, jnp.float32)
            for _ in range(j):
                value = value * rate
            for _ in range(n - j):
                value = value * stay
            power[n * (TOP + 1) + j] = value

    lane = lax.broadcasted_iota(jnp.int32, (8, LANES), 1)
    upper = lane >= 64
    odd = lane // 32 % 2 == 1
    power[0] = stay * ALPHA
    power[1] = rate * ALPHA

    def rotate(xs):
        return [xs[0]] + [pltpu.roll(xs[d], 32 * d, 1) for d in (1, 2, 3)]

    def take(g):
        left = g * GROUP
        held = []
        for q in range(QUADS):
            push = []
            for c in range(4):
                row = row_ref[left + 4 * q + c]
                theta = taken[0, pl.ds(row, 8, stride=8), :]
                moist = taken[1, pl.ds(row, 8, stride=8), :]
                held.append((moist - 0.2 * theta, theta + 0.5 * moist))
                push.append(jnp.broadcast_to(forcing_ref[pl.ds(column_ref[left + 4 * q + c], 1), :], (8, LANES)))
            held.append((0.2 * ALPHA) * jnp.where(upper, jnp.where(odd, push[3], push[2]), jnp.where(odd, push[1], push[0])))
        return held

    def put(held):
        for q in range(QUADS):
            quad = held[5 * q : 5 * q + 4]
            for d, x in enumerate(skew([x for x, _ in quad], odd, upper) + skew([x for _, x in quad], odd, upper)):
                stage[q * 9 + d] = x
            stage[q * 9 + 8] = held[5 * q + 4]

    def turn():
        return [
            (rotate([stage[q * 9 + d] for d in range(4)]), rotate([stage[q * 9 + 4 + d] for d in range(4)]), stage[q * 9 + 8])
            for q in range(QUADS)
        ]

    def keep(rolled):
        for q, (wet, dry, pull) in enumerate(rolled):
            wet, dry = skew(wet, odd, upper), skew(dry, odd, upper)
            for u in range(4):
                ready[q * 9 + u] = wet[-u % 4]
                ready[q * 9 + 4 + u] = dry[-u % 4]
            ready[q * 9 + 8] = pull

    gain = 0.725 / ALPHA
    floor = ALPHA * ALPHA * 0.01

    def drift(n):
        for q in range(QUADS):
            dry = [[ready[q * 9 + 4 + u] for u in range(4)]]
            dry.append([pltpu.roll(x, 1, 0) for x in dry[0]])
            if n > 4:
                dry.append([pltpu.roll(x, 2, 0) for x in dry[0]])
            shift = (n / (1.1 * 0.2 * ALPHA)) * ready[q * 9 + 8] - 0.5 / 1.1
            for u in range(4):
                total = shift
                for j in range(n + 1):
                    wraps = (j - u + 3) // 4 if j > u else 0
                    total = total + power[n * (TOP + 1) + j] * dry[wraps][(u - j) % 4]
                mid[q * 4 + u] = total

    def begin():
        wet = [[ready[q * 9 + u] for u in range(4)] for q in range(QUADS)]
        pull = [ready[q * 9 + 8] for q in range(QUADS)]
        return wet, pull

    def react(n, wet, pull):
        wet = list(wet)
        for s in range(n):
            keep_rate, move_rate = power[0], power[1]
            for q in range(QUADS):
                w = wet[q]
                less = pull[q] + ALPHA if s == 0 else pull[q]
                back = [pltpu.roll(w[3], 1, 0), w[0], w[1], w[2]]
                fresh = []
                for u in range(4):
                    e = keep_rate * w[u] + move_rate * back[u] - less
                    y = e * e + floor
                    fresh.append(gain * e - y * lax.rsqrt(y))
                wet[q] = fresh
        return wet

    def finish(wet):
        for q in range(QUADS):
            theta = [mid[q * 4 + u] - (0.5 / 1.1) * wet[q][u] for u in range(4)]
            moist = [wet[q][u] + 1.0 + 0.2 * theta[u] for u in range(4)]
            for d, x in enumerate(skew(theta, odd, upper) + skew(moist, odd, upper)):
                done[q * 8 + d] = x

    def store(g):
        left = g * GROUP
        for q in range(QUADS):
            for field in range(2):
                xs = skew(rotate([done[q * 8 + 4 * field + d] for d in range(4)]), odd, upper)
                for c in range(4):
                    given[field, pl.ds(row_ref[left + 4 * q + c], 8, stride=8), :] = xs[-c % 4]

    for copy in fetch(0):
        copy.wait()
    put(take(jnp.int32(0)))
    keep(turn())
    put(take(jnp.int32(1)))
    nothing = column_ref.shape[0] // GROUP - 1

    def chunk(k, last):
        for i in range(chunks - 1):
            @pl.when(k == i)
            def _(i=i):
                for copy in fetch(i + 1):
                    copy.wait()

        for n in range(1, TOP + 1):
            start, stop = bound_ref[k, n - 1], bound_ref[k, TOP + n - 1]

            def body(g, last, n=n):
                held = take(g + 2)
                rolled = turn()
                wet, pull = begin()
                drift(n)
                put(held)
                keep(rolled)
                store(last)
                finish(react(n, wet, pull))
                return g

            last = lax.fori_loop(start, stop, body, last)

            for i in range(chunks - 1):
                @pl.when((k == i + 1) & (start == bound_ref[k, 0]) & (stop > start))
                def _(i=i):
                    for copy in send(i):
                        copy.start()

        return last

    last = lax.fori_loop(0, chunks, chunk, jnp.int32(nothing))
    store(last)
    for copy in send(chunks - 1):
        copy.start()
    for k in range(chunks):
        for copy in send(k):
            copy.wait()


def shards(cloud_state, counts, courant, truncation):
    lon_devices = lax.axis_size("lon")
    fields, lon_local, lat_local, cells = cloud_state.shape
    pieces = cells // LANES
    columns = lon_local * lat_local
    chunks = len(chunk_ends(lon_local))
    slots = columns + chunks * TOP * (GROUP - 1) + 3 * GROUP
    highs = -(-slots // (8 * LANES)) * 8
    vmem = pl.BlockSpec(memory_space=pltpu.VMEM)
    smem = pl.BlockSpec(memory_space=pltpu.SMEM)
    column, row, bound = pl.pallas_call(
        order_kernel,
        in_specs=[vmem],
        out_specs=[vmem, vmem, vmem],
        out_shape=[
            jax.ShapeDtypeStruct((highs, LANES), jnp.int32),
            jax.ShapeDtypeStruct((highs, LANES), jnp.int32),
            jax.ShapeDtypeStruct((chunks, LANES), jnp.int32),
        ],
        compiler_params=pltpu.CompilerParams(vmem_limit_bytes=16 << 20),
        name="order",
    )(counts)
    pack = LANES // lat_local
    heating = pl.pallas_call(
        heating_kernel,
        in_specs=[pl.BlockSpec(memory_space=pl.ANY)],
        out_specs=vmem,
        out_shape=jax.ShapeDtypeStruct((lon_local // pack, LANES), jnp.float32),
        scratch_shapes=[
            pltpu.VMEM((lon_local, lat_local, cells), jnp.float32),
            pltpu.SemaphoreType.DMA((lon_local // 4,)),
        ],
        compiler_params=pltpu.CompilerParams(vmem_limit_bytes=50 << 20),
        name="heating",
    )(cloud_state)
    where = jnp.stack([lax.axis_index("lon"), lax.axis_index("lat")]).astype(jnp.int32)
    waves, table, rows = pl.pallas_call(
        functools.partial(tables_kernel, lon_devices=lon_devices, lon_local=lon_local),
        in_specs=[smem, vmem, vmem],
        out_specs=[vmem, vmem, vmem],
        out_shape=[
            jax.ShapeDtypeStruct((pack, lon_devices * lon_local // pack, 2 * LANES), jnp.float32),
            jax.ShapeDtypeStruct((NN, lat_local, LANES), jnp.float32),
            jax.ShapeDtypeStruct((8, LANES), jnp.float32),
        ],
        compiler_params=pltpu.CompilerParams(vmem_limit_bytes=16 << 20),
        name="tables",
    )(where, truncation[None], courant[None])
    mine, others = gather_heating(heating, lon_devices)
    tiles = cloud_state.reshape(fields, lon_local, lat_local // 8, 8, pieces, LANES)
    tiles = tiles.transpose(0, 1, 2, 4, 3, 5).reshape(fields, columns * pieces, LANES)
    held_rows = columns * pieces + 8 * pieces
    out = pl.pallas_call(
        functools.partial(cloud_kernel, lon_local=lon_local),
        in_specs=[smem, smem, smem, smem, pl.BlockSpec(memory_space=pl.ANY)] + [vmem] * 5,
        out_specs=pl.BlockSpec(memory_space=pl.ANY),
        out_shape=jax.ShapeDtypeStruct(tiles.shape, jnp.float32),
        scratch_shapes=[
            pltpu.VMEM((fields, held_rows, LANES), jnp.float32),
            pltpu.VMEM((fields, held_rows, LANES), jnp.float32),
            pltpu.VMEM((columns + 8, LANES), jnp.float32),
            pltpu.VMEM((2, NN, 8, LANES), jnp.float32),
            pltpu.VMEM((QUADS * 9, 8, LANES), jnp.float32),
            pltpu.VMEM((QUADS * 9, 8, LANES), jnp.float32),
            pltpu.VMEM((QUADS * 4, 8, LANES), jnp.float32),
            pltpu.VMEM((QUADS * 8, 8, LANES), jnp.float32),
            pltpu.VMEM(((TOP + 1) ** 2, 8, LANES), jnp.float32),
            pltpu.SemaphoreType.DMA((chunks, 1)),
            pltpu.SemaphoreType.DMA((chunks, 1)),
        ],
        compiler_params=pltpu.CompilerParams(vmem_limit_bytes=44 << 20),
        name="clouds",
    )(column.reshape(-1), row.reshape(-1), bound, where, tiles, mine, others, rows, waves, table)
    out = out.reshape(fields, lon_local, lat_local // 8, pieces, 8, LANES)
    return out.transpose(0, 1, 2, 4, 3, 5).reshape(cloud_state.shape)


def solution(mesh):
    return jax.shard_map(
        shards,
        mesh=mesh,
        in_specs=(P("grp", "lon", "lat", None), P(("grp", "lon"), "lat"), P(), P()),
        out_specs=P("grp", "lon", "lat", None),
        check_vma=False,
    )
```
